32 devices in a mesh: dp: 8 (over y, x, core), mp: 4 (over z).
Axes of the slice: x: 2, y: 2, z: 4, core: 2. Of those that a mesh axis runs over, the one named last changes fastest.
Arguments:
- tokens: bfloat16 [8192, 640], P(('dp', 'mp')), may hold values from -6 to 6
- lengths: int32 [8], P('dp'), may hold values from 20 to 1024, as said below
- key_keep: int32 [8, 1024], P('dp'), may hold values 0 or 1
- ln_gain: float32 [2, 2, 640], replicated, may hold values from 0.25 to 1.75
- ln_bias: float32 [2, 2, 640], replicated, may hold values from -1.5 to 1.5
- w_qkv: bfloat16 [2, 640, 3, 640], P(None, None, None, 'mp'), may hold values from -0.25 to 0.25
- w_out: bfloat16 [2, 640, 640], P(None, 'mp'), may hold values from -1 to 1
- w_up: bfloat16 [2, 640, 5120], P(None, None, 'mp'), may hold values from -0.25 to 0.25
- w_down: bfloat16 [2, 5120, 640], P(None, 'mp'), may hold values from -0.078125 to 0.078125
- readout: bfloat16 [640, 25], replicated, may hold values from -0.5 to 0.5
- labels: int32 [8192], P(('dp', 'mp')), may hold values from 0 to 24
- cotangent: bfloat16 [8192, 640], P(('dp', 'mp')), may hold values from -6 to 6
Outputs:
- layer_out: bfloat16 [8192, 640], P(('dp', 'mp'))
- grad_tokens: float32 [8192, 640], P(('dp', 'mp'))
- grad_ln_gain: float32 [2, 2, 640], replicated
- grad_ln_bias: float32 [2, 2, 640], replicated
- grad_w_qkv: float32 [2, 640, 3, 640], P(None, None, None, 'mp')
- grad_w_out: float32 [2, 640, 640], P(None, 'mp')
- grad_w_up: float32 [2, 640, 5120], P(None, None, 'mp')
- grad_w_down: float32 [2, 5120, 640], P(None, 'mp')
- label_logprob: float32 [8192], P(('dp', 'mp'))
- token_count: int32 [], replicated
The draws below stay inside these ranges and needn't reach their ends.
Inputs may be any that keep to these rules, and one draw needn't show every extreme that they name: `lengths`: each sequence's true length; in every draw some sequence has length exactly 1024.
All inputs are finite; a program needn't handle non-finite values. No bound on the sum of `key_keep` on one device may be relied on, other than what follows from the above.
Results may differ from the reference program's by a relative error of at most 0.017.
Values may be sent and summed in bfloat16 or wider, within the bound.
No kernel may reach another device: no remote copies, remote signals or barrier semaphores. Data moves between devices by JAX's collectives and lax.ppermute only.
A program may use at most 192 MiB of HBM per device.

```python
import math
import jax
import jax.numpy as jnp
from jax import lax

D = 640
H = 20
HD = 32
FF = 5120
VOCAB = 25
SEQ_LEN = 1024
MINLEN = 20
LAYERS = 2
NSEQ = 8
TOKENS = 8192


def draw_lengths(key, part):
    first_key, second_key = jax.random.split(key)
    values = jax.random.randint(first_key, (NSEQ,), MINLEN, SEQ_LEN + 1)
    chosen_one = jax.random.randint(second_key, (), 0, NSEQ)
    return jnp.where(jnp.arange(NSEQ) == chosen_one, SEQ_LEN, values).astype(jnp.int32)


def draw_cotangent(key, part):
    noise_key = jax.random.fold_in(jax.random.fold_in(key, 17), 0)
    noise = jax.random.normal(noise_key, (TOKENS, D), jnp.float32)
    values = noise
    return jnp.clip(values, -6.0, 6.0).astype(jnp.bfloat16)


def touch_ends(drawn, stream_key, low, high):
    longest = drawn.shape.index(max(drawn.shape))
    spots = []
    for shift in (0, 1):
        where = [jax.random.randint(jax.random.fold_in(stream_key, axis), (), 0, length) for axis, length in enumerate(drawn.shape)]
        where[longest] = (where[longest] + shift) % drawn.shape[longest]
        spots.append(tuple(where))
    return drawn.at[spots[0]].set(low).at[spots[1]].set(high)


def level_of(rng, dims, pieces, smallest, largest):
    def one(position, shards_of):
        draws = jax.random.uniform(jax.random.fold_in(jax.random.fold_in(rng, 6), position), (shards_of,), jnp.float32, smallest / len(pieces), largest / len(pieces))
        return jnp.repeat(jnp.exp(draws), dims[position] // shards_of).reshape((-1,) + (1,) * (len(dims) - position - 1))

    level = one(*pieces[0])
    for cut in pieces[1:]:
        level = level * one(*cut)
    return level


def gaussian(key, dims, scale, most, pieces=(), kind=jnp.bfloat16):
    loudness = level_of(key, dims, pieces, -0.22, 0.18) if pieces else 1.0
    values = jax.random.normal(key, dims, jnp.float32) * scale * loudness
    return jnp.minimum(jnp.maximum(values, -most), most).astype(kind)


def setup_inputs(seed: int = 0) -> dict:
    streams_of = jax.random.split(jax.random.key(seed), 13)
    return {
        "tokens": gaussian(streams_of[0], (TOKENS, D), 1.0, 6.0, ((0, 32),)),
        "lengths": draw_lengths(jax.random.fold_in(streams_of[12], 71), 0),
        "key_keep": touch_ends((jax.random.randint(streams_of[2], (NSEQ, SEQ_LEN), 0, 8) < 7).astype(jnp.int32), jax.random.fold_in(streams_of[2], 1), 0, 1),
        "ln_gain": jnp.clip(1.0 + 0.15 * jax.random.normal(streams_of[3], (LAYERS, 2, D), jnp.float32), 0.25, 1.75),
        "ln_bias": gaussian(streams_of[4], (LAYERS, 2, D), 0.3, 1.5, (), jnp.float32),
        "w_qkv": gaussian(streams_of[5], (LAYERS, D, 3, D), D ** -0.5, 0.25, ((3, 4),)),
        "w_out": gaussian(streams_of[6], (LAYERS, D, D), (D // 16) ** -0.5, 1.0, ((1, 4),)),
        "w_up": gaussian(streams_of[7], (LAYERS, D, FF), D ** -0.5, 0.25, ((2, 4),)),
        "w_down": gaussian(streams_of[8], (LAYERS, FF, D), FF ** -0.5, 0.078125, ((1, 4),)),
        "readout": gaussian(streams_of[9], (D, VOCAB), (D // 4) ** -0.5, 0.5),
        "labels": touch_ends(jax.random.randint(streams_of[10], (TOKENS,), 0, VOCAB), jax.random.fold_in(streams_of[10], 1), 0, VOCAB - 1).astype(jnp.int32),
        "cotangent": draw_cotangent(jax.random.fold_in(streams_of[12], 71), 0),
    }


EPS = 1e-05
NEG = -1000000000.0
ROOT_HALF = 0.7071067811865476

@jax.custom_vjp
def low(v):
    return lax.optimization_barrier(v.astype(jnp.bfloat16)).astype(jnp.float32)

@jax.custom_vjp
def low_back(v):
    return v

def low_keep(v):
    return (low(v), None)

def low_pass(kept, grad):
    return (grad,)

def back_keep(v):
    return (v, None)

def back_low(kept, grad):
    return (low(grad),)
low.defvjp(low_keep, low_pass)
low_back.defvjp(back_keep, back_low)

def layer_norm(values, gain, shift):
    mean = lax.optimization_barrier(jnp.mean(values, axis=-1, keepdims=True))
    centred = values - mean
    spread = lax.optimization_barrier(jnp.mean(centred * centred, axis=-1, keepdims=True))
    return centred * lax.rsqrt(spread + EPS) * gain + shift

def gelu_value(values):
    return 0.5 * values * (1.0 + lax.erf(values * ROOT_HALF))

def attention(queries, keys_all, values, allowed):
    block = min(512, SEQ_LEN)
    scale = 1.0 / math.sqrt(HD)
    col_ids = jnp.arange(SEQ_LEN, dtype=jnp.int32)

    def one_block(first):
        query_blk = lax.dynamic_slice_in_dim(queries, first, block, 1)
        scores = low_back(jnp.einsum('gqhd,gkhd->ghqk', query_blk, keys_all, precision=lax.Precision.HIGHEST) * scale)
        row_ids = first + jnp.arange(block, dtype=jnp.int32)
        permitted = allowed[:, None, None, :] | (row_ids[:, None] == col_ids[None, :])[None, None]
        scores = jnp.where(permitted, scores, NEG)
        top = lax.optimization_barrier(jnp.max(scores, axis=-1, keepdims=True))
        expo = jnp.exp(scores - top)
        probs = low(expo / lax.optimization_barrier(jnp.sum(expo, axis=-1, keepdims=True)))
        return jnp.einsum('ghqk,gkhd->gqhd', probs, values, precision=lax.Precision.HIGHEST)
    starts = (jnp.arange(SEQ_LEN // block, dtype=jnp.int32) * block).astype(jnp.int32)
    outputs = lax.map(jax.checkpoint(one_block), starts)
    return jnp.moveaxis(outputs, 0, 1).reshape(queries.shape)

def forward(inputs, allowed, params):
    ln_gain, ln_bias, w_qkv, w_out, w_up, w_down = params
    groups = inputs.shape[0]
    hidden = inputs.reshape(groups * SEQ_LEN, D)
    for depth in range(LAYERS):
        normed = low(layer_norm(hidden, ln_gain[depth, 0], ln_bias[depth, 0]))
        mixed = jnp.dot(normed, w_qkv[depth].reshape(D, 3 * D), precision=lax.Precision.HIGHEST)
        mixed = mixed.reshape(groups, SEQ_LEN, 3, H, HD)
        queries = low_back(low(mixed[:, :, 0]))
        keys_all = low_back(low(mixed[:, :, 1]))
        values = low_back(low(mixed[:, :, 2]))
        attended = low_back(low(attention(queries, keys_all, values, allowed)))
        branch = low_back(jnp.dot(attended.reshape(groups * SEQ_LEN, D), w_out[depth], precision=lax.Precision.HIGHEST))
        hidden = hidden + branch
        normed_two = low(layer_norm(hidden, ln_gain[depth, 1], ln_bias[depth, 1]))
        pre_act = low_back(jnp.dot(normed_two, w_up[depth], precision=lax.Precision.HIGHEST))
        activated = low(gelu_value(pre_act))
        branch_two = low_back(jnp.dot(activated, w_down[depth], precision=lax.Precision.HIGHEST))
        hidden = hidden + branch_two
    return hidden.reshape(groups, SEQ_LEN, D)

def reference(tokens, lengths, key_keep, ln_gain, ln_bias, w_qkv, w_out, w_up, w_down, readout, labels, cotangent):
    nseq = lengths.shape[0]
    group = math.gcd(nseq, 4)
    col_ids = jnp.arange(SEQ_LEN, dtype=jnp.int32)
    allowed = (col_ids[None, :] < lengths[:, None]) & (key_keep == 1)
    params = (ln_gain.astype(jnp.float32), ln_bias.astype(jnp.float32), w_qkv.astype(jnp.float32), w_out.astype(jnp.float32), w_up.astype(jnp.float32), w_down.astype(jnp.float32))
    inputs = tokens.astype(jnp.float32).reshape(nseq // group, group, SEQ_LEN, D)
    cots = cotangent.astype(jnp.float32).reshape(nseq // group, group, SEQ_LEN, D)
    masks = allowed.reshape(nseq // group, group, SEQ_LEN)

    def step(acc, items):
        x_group, cot_group, mask_group = items

        def run(xx, pp):
            return forward(xx, mask_group, pp)
        result, pull = jax.vjp(run, x_group, params)
        grad_x, grad_p = pull(cot_group)
        return (jax.tree.map(lambda s, t: s + t, acc, grad_p), (result, grad_x))
    zeros = jax.tree.map(jnp.zeros_like, params)
    sums, (results, grads) = lax.scan(step, zeros, (inputs, cots, masks))
    layer_out = results.reshape(TOKENS, D).astype(jnp.bfloat16)
    grad_tokens = grads.reshape(TOKENS, D)
    logits = jnp.dot(layer_out, readout, preferred_element_type=jnp.float32)
    top = lax.optimization_barrier(jnp.max(logits, axis=-1, keepdims=True))
    log_total = top[:, 0] + jnp.log(lax.optimization_barrier(jnp.sum(jnp.exp(logits - top), axis=-1)))
    classes = jnp.arange(VOCAB, dtype=jnp.int32)
    picked = lax.optimization_barrier(jnp.sum(jnp.where(labels[:, None] == classes[None, :], logits, 0.0), axis=-1))
    live = (col_ids[None, :] < lengths[:, None]).reshape(TOKENS)
    label_logprob = jnp.where(live, picked - log_total, jnp.zeros_like(log_total))
    token_count = jnp.sum(lengths).astype(jnp.int32)
    return (layer_out, grad_tokens, sums[0], sums[1], sums[2], sums[3], sums[4], sums[5], label_logprob, token_count)
```

```python
import math

import jax
import jax.numpy as jnp
from jax import lax
from jax.sharding import Mesh, PartitionSpec as P

HD = 32
LAYERS = 2


EPS = 1e-05
NEG = -1000000000.0
ROOT_HALF = 0.7071067811865476
INV_ROOT_TAU = 0.3989422804014327

BF = jnp.bfloat16
F32 = jnp.float32
FLIP = [(0, 1), (1, 0)]

HOME = []
for _c in range(2):
    for _h in range(2):
        for _p in range(2):
            _to = (_c, _h, _p) if _c == _h else (1 - _c, 1 - _h, _p)
            HOME.append((4 * _c + 2 * _h + _p, 4 * _to[0] + 2 * _to[1] + _to[2]))


def rehome(x):
    return lax.ppermute(x, ("c", "zh", "zl"), HOME)


def flip(x, axis):
    return lax.ppermute(x, axis, FLIP)


def norm_forward(values, gain, shift):
    mean = jnp.mean(values, axis=-1, keepdims=True)
    centred = values - mean
    spread = jnp.mean(centred * centred, axis=-1, keepdims=True)
    inverse = lax.rsqrt(spread + EPS)
    unit = centred * inverse
    return (unit * gain + shift, unit, inverse)


def norm_backward(grad_out, unit, inverse, gain):
    scaled = grad_out * gain
    mean_one = jnp.mean(scaled, axis=-1, keepdims=True)
    mean_two = jnp.mean(scaled * unit, axis=-1, keepdims=True)
    grad_in = inverse * (scaled - mean_one - unit * mean_two)
    return (grad_in, jnp.sum(grad_out * unit, axis=0), jnp.sum(grad_out, axis=0))


def gelu_value(values):
    return 0.5 * values * (1.0 + lax.erf(values * ROOT_HALF))


def gelu_slope(values):
    return (
        0.5 * (1.0 + lax.erf(values * ROOT_HALF))
        + values * jnp.exp(-0.5 * values * values) * INV_ROOT_TAU
    )


def dot(left, right):
    return jnp.dot(left, right, preferred_element_type=F32)


def group_gather(x):
    plane = flip(x, "zl")
    core = flip(x, "c")
    both = flip(plane, "c")
    return jnp.concatenate([x, core, plane, both], axis=0)


def group_scatter(x):
    rows = x.shape[0] // 4
    x = x.astype(BF)
    both = flip(x[3 * rows :], "c")
    plane = (x[2 * rows : 3 * rows].astype(F32) + both.astype(F32)).astype(BF)
    plane = flip(plane, "zl")
    core = flip(x[rows : 2 * rows], "c")
    return x[:rows].astype(F32) + core.astype(F32) + plane.astype(F32)


def spread_rest(x, count):
    return lax.all_to_all(jnp.broadcast_to(x[None], (count,) + x.shape), "r", 0, 0)


def sum_rest(x):
    return jnp.sum(lax.all_to_all(x.astype(BF), "r", 0, 0).astype(F32), axis=0)


def masked_scores(query_blk, keys_all, allowed, first, scale):
    scores = (
        jnp.einsum("qhd,khd->hqk", query_blk, keys_all, preferred_element_type=jnp.float32)
        * scale
    )
    row_ids = first + jnp.arange(query_blk.shape[0], dtype=jnp.int32)
    col_ids = jnp.arange(keys_all.shape[0], dtype=jnp.int32)
    permitted = allowed[None, None, :] | (row_ids[:, None] == col_ids[None, :])[None]
    return jnp.where(permitted, scores, NEG)


def attend_forward(queries, keys_all, values, allowed, block_rows, scale):
    outputs = []
    totals = []
    for first in range(0, queries.shape[0], block_rows):
        query_blk = queries[first : first + block_rows]
        scores = masked_scores(query_blk, keys_all, allowed, first, scale)
        top = jnp.max(scores, axis=-1, keepdims=True)
        expo = jnp.exp(scores - top)
        total = jnp.sum(expo, axis=-1, keepdims=True)
        probs = (expo / total).astype(BF)
        outputs.append(
            jnp.einsum("hqk,khd->qhd", probs, values, preferred_element_type=F32).astype(BF)
        )
        totals.append(top + jnp.log(total))
    return (jnp.concatenate(outputs, axis=0), jnp.concatenate(totals, axis=1))


def attend_backward(queries, keys_all, values, out_grad, log_totals, allowed, block_rows, scale):
    key_acc = jnp.zeros(keys_all.shape, F32)
    value_acc = jnp.zeros(values.shape, F32)
    query_parts = []
    for first in range(0, queries.shape[0], block_rows):
        query_blk = queries[first : first + block_rows]
        grad_blk = out_grad[first : first + block_rows]
        scores = masked_scores(query_blk, keys_all, allowed, first, scale)
        probs = jnp.exp(scores - log_totals[:, first : first + block_rows])
        probs_low = probs.astype(BF)
        value_acc = value_acc + jnp.einsum(
            "hqk,qhd->khd", probs_low, grad_blk, preferred_element_type=F32
        )
        prob_grad = jnp.einsum("qhd,khd->hqk", grad_blk, values, preferred_element_type=F32)
        inner = jnp.sum(probs * prob_grad, axis=-1, keepdims=True)
        score_grad = (probs * (prob_grad - inner)).astype(BF)
        query_parts.append(
            (
                jnp.einsum("hqk,khd->qhd", score_grad, keys_all, preferred_element_type=F32) * scale
            ).astype(BF)
        )
        key_acc = (
            key_acc
            + jnp.einsum("hqk,qhd->khd", score_grad, query_blk, preferred_element_type=F32) * scale
        )
    return (
        jnp.concatenate(query_parts, axis=0),
        key_acc.astype(BF),
        value_acc.astype(BF),
    )


def local(
    tokens,
    lengths,
    key_keep,
    ln_gain,
    ln_bias,
    w_qkv,
    w_out,
    w_up,
    w_down,
    readout,
    labels,
    cotangent,
    *,
    rest,
):
    rows_shard, model_width = tokens.shape
    seq_len = key_keep.shape[1]
    local_width = w_qkv.shape[3]
    local_heads = local_width // HD
    hidden_local = w_up.shape[2]
    half = hidden_local // 2
    total_rows = 4 * rows_shard
    block_rows = min(512, seq_len)
    scale = 1.0 / math.sqrt(HD)
    r = lax.axis_index("r")
    c = lax.axis_index("c")
    zh = lax.axis_index("zh")
    zl = lax.axis_index("zl")
    at_home = c == zh
    slab = model_width // rest
    slab_half = half // rest

    hidden = rehome(tokens).astype(F32)
    mix_weights, out_weights, up_weights, down_weights = [], [], [], []
    for depth in range(LAYERS):
        mix_weights.append(rehome(w_qkv[depth].reshape(model_width, 3 * local_width)))
        out_weights.append(rehome(w_out[depth]))
        up_home = lax.dynamic_slice(w_up[depth], (0, c * half), (model_width, half))
        up_part = lax.dynamic_slice(w_up[depth], (r * slab, c * half), (slab, half))
        up_far = spread_rest(flip(up_part, "zh"), rest).reshape(model_width, half)
        up_weights.append(jnp.concatenate([up_home, up_far], axis=1))
        down_home = lax.dynamic_slice(w_down[depth], (c * half, 0), (half, model_width))
        down_part = lax.dynamic_slice(
            w_down[depth], (c * half + r * slab_half, 0), (slab_half, model_width)
        )
        down_far = spread_rest(flip(down_part, "zh"), rest).reshape(half, model_width)
        down_weights.append(jnp.concatenate([down_home, down_far], axis=0))
    cotangent_home = rehome(cotangent)

    col_ids = jnp.arange(seq_len, dtype=jnp.int32)
    allowed = ((col_ids[None, :] < lengths[:, None]) & (key_keep == 1)).astype(jnp.int32)
    allowed = jnp.where(at_home, allowed, flip(allowed, "c")).reshape(2, 2, rows_shard)
    allowed = jnp.where(c == 1, allowed[::-1], allowed)
    allowed = jnp.where(zl == 1, allowed[:, ::-1], allowed)
    allowed = jnp.swapaxes(allowed, 0, 1).reshape(seq_len) == 1

    saved = []
    for depth in range(LAYERS):
        normed_one, unit_one, inv_one = norm_forward(hidden, ln_gain[depth, 0], ln_bias[depth, 0])
        attn_input = group_gather(normed_one.astype(BF))
        mixed = dot(attn_input, mix_weights[depth])
        mixed = mixed.reshape(total_rows, 3, local_heads, HD).astype(BF)
        queries = mixed[:, 0]
        keys_all = mixed[:, 1]
        values = mixed[:, 2]
        attended, log_totals = attend_forward(queries, keys_all, values, allowed, block_rows, scale)
        attended_flat = attended.reshape(total_rows, local_width)
        middle = hidden + group_scatter(dot(attended_flat, out_weights[depth]))
        normed_two, unit_two, inv_two = norm_forward(middle, ln_gain[depth, 1], ln_bias[depth, 1])
        ffn_input = group_gather(normed_two.astype(BF))
        pre_act = dot(ffn_input, up_weights[depth])
        activated = gelu_value(pre_act).astype(BF)
        saved.append(
            (
                unit_one,
                inv_one,
                attn_input,
                queries,
                keys_all,
                values,
                attended_flat,
                log_totals,
                unit_two,
                inv_two,
                ffn_input,
                pre_act,
            )
        )
        hidden = middle + group_scatter(dot(activated, down_weights[depth]))

    layer_out = rehome(hidden.astype(BF))
    row_ids = (2 * zh + zl) * rows_shard + jnp.arange(rows_shard, dtype=jnp.int32)
    live_rows = row_ids < lengths[0]
    logits = dot(layer_out, readout)
    top = jnp.max(logits, axis=-1, keepdims=True)
    log_total = top[:, 0] + jnp.log(jnp.sum(jnp.exp(logits - top), axis=-1))
    classes = jnp.arange(logits.shape[1], dtype=jnp.int32)
    picked = jnp.sum(jnp.where(labels[:, None] == classes[None, :], logits, 0.0), axis=-1)
    label_logprob = jnp.where(live_rows, picked - log_total, jnp.zeros_like(log_total))

    grad = cotangent_home.astype(F32)
    grads_mix = [None] * LAYERS
    grads_out = [None] * LAYERS
    grads_up = [None] * LAYERS
    grads_down = [None] * LAYERS
    gains_back = [None] * LAYERS
    shifts_back = [None] * LAYERS
    for depth in reversed(range(LAYERS)):
        (
            unit_one,
            inv_one,
            attn_input,
            queries,
            keys_all,
            values,
            attended_flat,
            log_totals,
            unit_two,
            inv_two,
            ffn_input,
            pre_act,
        ) = saved[depth]
        down_rows = group_gather(grad.astype(BF))
        activated = gelu_value(pre_act).astype(BF)
        act_grad = dot(down_rows, down_weights[depth].T)
        pre_grad = (act_grad * gelu_slope(pre_act)).astype(BF)
        norm_grad_two = group_scatter(dot(pre_grad, up_weights[depth].T))
        grad_down = dot(activated.T, down_rows)
        grad_up = dot(ffn_input.T, pre_grad)
        back_two, gain_two, shift_two = norm_backward(
            norm_grad_two, unit_two, inv_two, ln_gain[depth, 1]
        )
        grad = grad + back_two

        part = sum_rest(grad_up.reshape(rest, slab, hidden_local))
        part = part[:, :half] + flip(part[:, half:].astype(BF), "zh").astype(F32)
        mine = spread_rest(part.astype(BF), rest).reshape(model_width, half)
        other = flip(mine, "c")
        grads_up[depth] = jnp.where(
            c == 0,
            jnp.concatenate([mine, other], axis=1),
            jnp.concatenate([other, mine], axis=1),
        ).astype(F32)
        part = grad_down.reshape(2, rest, slab_half, model_width)
        part = sum_rest(jnp.swapaxes(part, 0, 1))
        part = part[0] + flip(part[1].astype(BF), "zh").astype(F32)
        mine = spread_rest(part.astype(BF), rest).reshape(half, model_width)
        other = flip(mine, "c")
        grads_down[depth] = jnp.where(
            c == 0,
            jnp.concatenate([mine, other], axis=0),
            jnp.concatenate([other, mine], axis=0),
        ).astype(F32)

        out_rows = group_gather(grad.astype(BF))
        attended_grad = dot(out_rows, out_weights[depth].T).astype(BF)
        attended_grad = attended_grad.reshape(total_rows, local_heads, HD)
        query_grad, key_grad, value_grad = attend_backward(
            queries, keys_all, values, attended_grad, log_totals, allowed, block_rows, scale
        )
        mix_grad = jnp.stack([query_grad, key_grad, value_grad], axis=1).reshape(
            total_rows, 3 * local_width
        )
        norm_grad_one = group_scatter(dot(mix_grad, mix_weights[depth].T))
        grad_out = dot(attended_flat.T, out_rows)
        grad_mix = dot(attn_input.T, mix_grad)
        for grad_weight, store in ((grad_out, grads_out), (grad_mix, grads_mix)):
            shape = grad_weight.shape
            part = sum_rest(grad_weight.reshape((rest, shape[0] // rest) + shape[1:]))
            part = part.astype(BF)
            part = (part.astype(F32) + flip(part, "zh").astype(F32)).astype(BF)
            mine = spread_rest(part, rest).reshape(shape)
            store[depth] = jnp.where(at_home, mine, flip(mine, "c")).astype(F32)
        back_one, gain_one, shift_one = norm_backward(
            norm_grad_one, unit_one, inv_one, ln_gain[depth, 0]
        )
        grad = grad + back_one
        gains_back[depth] = jnp.stack([gain_one, gain_two])
        shifts_back[depth] = jnp.stack([shift_one, shift_two])
    grad_tokens = rehome(grad.astype(BF)).astype(F32)
    everyone = ("r", "c", "zh", "zl")
    devices = 8 * rest
    small = jnp.stack([jnp.stack(gains_back), jnp.stack(shifts_back)])
    small = jnp.broadcast_to(small[None], (devices,) + small.shape)
    small = jnp.sum(lax.all_to_all(small, everyone, 0, 0), axis=0)
    token_count = lax.psum(jnp.sum(lengths), ("r", "c"))
    return (
        layer_out,
        grad_tokens,
        small[0],
        small[1],
        jnp.stack(grads_mix).reshape(LAYERS, model_width, 3, local_width),
        jnp.stack(grads_out),
        jnp.stack(grads_up),
        jnp.stack(grads_down),
        label_logprob,
        token_count,
    )


def solution(mesh):
    batch, model = mesh.devices.shape
    rest = batch // 2
    fine = Mesh(mesh.devices.reshape(rest, 2, 2, model // 2), ("r", "c", "zh", "zl"))
    dp = ("r", "c")
    mp = ("zh", "zl")
    both = dp + mp
    in_specs = (
        P(both, None),
        P(dp),
        P(dp, None),
        P(),
        P(),
        P(None, None, None, mp),
        P(None, mp, None),
        P(None, None, mp),
        P(None, mp, None),
        P(),
        P(both),
        P(both, None),
    )
    out_specs = (
        P(both, None),
        P(both, None),
        P(),
        P(),
        P(None, None, None, mp),
        P(None, mp, None),
        P(None, None, mp),
        P(None, mp, None),
        P(both),
        P(),
    )

    def body(*args):
        return local(*args, rest=rest)

    return jax.shard_map(body, mesh=fine, in_specs=in_specs, out_specs=out_specs, check_vma=False)
```

```python
import functools
import math

import jax
import jax.numpy as jnp
from jax import lax
from jax.experimental import pallas as pl
from jax.experimental.pallas import tpu as pltpu
from jax.sharding import Mesh, PartitionSpec as P

HD = 32
LAYERS = 2


EPS = 1e-05
NEG = -1000000000.0
ROOT_HALF = 0.7071067811865476
INV_ROOT_TAU = 0.3989422804014327
LOG2_E = 1.4426950408889634
VMEM_LIMIT = 56 * 1024 * 1024

BF = jnp.bfloat16
F32 = jnp.float32
FLIP = [(0, 1), (1, 0)]

HOME = []
for _c in range(2):
    for _h in range(2):
        for _p in range(2):
            _to = (_c, _h, _p) if _c == _h else (1 - _c, 1 - _h, _p)
            HOME.append((4 * _c + 2 * _h + _p, 4 * _to[0] + 2 * _to[1] + _to[2]))


def rehome(x):
    return lax.ppermute(x, ("c", "zh", "zl"), HOME)


def flip(x, axis):
    return lax.ppermute(x, axis, FLIP)


def tie(x, *before):
    return lax.optimization_barrier((x, before))[0]


def whole(*shape):
    return pl.BlockSpec(shape, lambda *_: (0,) * len(shape))


def kernel_params(micros):
    return dict(
        compiler_params=pltpu.CompilerParams(vmem_limit_bytes=VMEM_LIMIT),
        cost_estimate=pl.CostEstimate(
            flops=int(micros * 1.15e9), bytes_accessed=1 << 20, transcendentals=0
        ),
    )


def norm_unit(values):
    mean = jnp.mean(values, axis=-1, keepdims=True)
    centred = values - mean
    spread = jnp.mean(centred * centred, axis=-1, keepdims=True)
    inverse = lax.rsqrt(spread + EPS)
    return centred * inverse, inverse


def norm_forward_kernel(count, hidden_ref, *refs):
    parts = refs[:count]
    gain_ref, bias_ref, sum_ref, normed_ref = refs[count:]
    values = hidden_ref[...].astype(F32)
    for part in parts:
        values = values + part[...].astype(F32)
    sum_ref[...] = values
    unit, _ = norm_unit(values)
    normed_ref[...] = (unit * gain_ref[...] + bias_ref[...]).astype(BF)


def norm_forward(hidden, parts, gain, bias):
    rows, model = hidden.shape
    return pl.pallas_call(
        functools.partial(norm_forward_kernel, len(parts)),
        out_shape=[
            jax.ShapeDtypeStruct((rows, model), F32),
            jax.ShapeDtypeStruct((rows, model), BF),
        ],
        name="norm_forward",
        **kernel_params(2.5),
    )(hidden, *parts, gain[None], bias[None])


def norm_backward_kernel(
    own_ref, core_ref, plane_ref, values_ref, grad_ref, gain_ref, out_ref, low_ref, sums_ref
):
    grad_normed = own_ref[...].astype(F32) + core_ref[...].astype(F32) + plane_ref[...].astype(F32)
    unit, inverse = norm_unit(values_ref[...])
    scaled = grad_normed * gain_ref[...]
    mean_one = jnp.mean(scaled, axis=-1, keepdims=True)
    mean_two = jnp.mean(scaled * unit, axis=-1, keepdims=True)
    grad = grad_ref[...].astype(F32) + inverse * (scaled - mean_one - unit * mean_two)
    out_ref[...] = grad
    low_ref[...] = grad.astype(BF)
    sums_ref[0:1, :] = jnp.sum(grad_normed * unit, axis=0, keepdims=True)
    sums_ref[1:2, :] = jnp.sum(grad_normed, axis=0, keepdims=True)


def norm_backward(parts, values, grad, gain):
    rows, model = values.shape
    return pl.pallas_call(
        norm_backward_kernel,
        out_shape=[
            jax.ShapeDtypeStruct((rows, model), F32),
            jax.ShapeDtypeStruct((rows, model), BF),
            jax.ShapeDtypeStruct((2, model), F32),
        ],
        name="norm_backward",
        **kernel_params(3),
    )(*parts, values, grad, gain[None])


def gelu_and_slope(u):
    cdf = 0.5 * (1.0 + lax.erf(u * ROOT_HALF))
    return (u * cdf).astype(BF), cdf + u * jnp.exp(-0.5 * u * u) * INV_ROOT_TAU


def ffn_forward(x, up_w, down_w):
    u = dot(x, up_w)
    act = gelu_and_slope(u)[0]
    return dot(act, down_w).astype(BF), act, u


def ffn_backward(x, up_w, down_w, u):
    grad = (dot_nt(x, down_w) * gelu_and_slope(u)[1]).astype(BF)
    return dot_nt(grad, up_w).astype(BF), grad


def dot(left, right):
    return jnp.dot(left, right, preferred_element_type=F32)


def gather_start(x):
    plane = flip(x, "zl")
    return x, flip(x, "c"), plane, flip(plane, "c")


def scatter_far(plane, both):
    both = flip(both, "c")
    sent = (plane.astype(F32) + both.astype(F32)).astype(BF)
    return sent, flip(sent, "zl")


def exchange_rest(x):
    return lax.all_to_all(x, "r", 0, 0)


def spread_rest(x, count):
    return exchange_rest(jnp.broadcast_to(x[None], (count,) + x.shape))


def permute_rest(x, count):
    if count != 4:
        return spread_rest(x, count)
    r = lax.axis_index("r")
    pieces = [x] + [lax.ppermute(x, "r", [(i, i ^ k) for i in range(count)]) for k in range(1, count)]
    pieces = jnp.stack(pieces)
    return jnp.stack([lax.dynamic_index_in_dim(pieces, r ^ k, keepdims=False) for k in range(count)])


def weights_kernel(place_ref, up_home_ref, down_home_ref, far_ref, up_ref, down_ref):
    slab, half = up_home_ref.shape[1:]
    up_ref[:, :half] = up_home_ref[0]
    up_ref[:, half:] = far_ref[0, :slab]
    down_ref[0] = down_home_ref[0, 0]
    down_ref[1] = far_ref[0, slab:]


def ffn_weights_here(depth, place, w_up, w_down, far):
    model, hidden_local = w_up.shape[1:]
    half = hidden_local // 2
    count, span = far.shape[:2]
    slab, rows = model // count, half // count
    up, down = pl.pallas_call(
        weights_kernel,
        grid_spec=pltpu.PrefetchScalarGridSpec(
            num_scalar_prefetch=1,
            grid=(count,),
            in_specs=[
                pl.BlockSpec((1, slab, half), lambda j, p: (depth, j, p[0])),
                pl.BlockSpec((1, 1, rows, model), lambda j, p: (depth, p[0], j, 0)),
                pl.BlockSpec((1, span, model), lambda j, p: (j, 0, 0)),
            ],
            out_specs=[
                pl.BlockSpec((slab, hidden_local), lambda j, p: (j, 0)),
                pl.BlockSpec((2, rows, model), lambda j, p: (0, j, 0)),
            ],
        ),
        out_shape=[
            jax.ShapeDtypeStruct((model, hidden_local), BF),
            jax.ShapeDtypeStruct((2, half, model), BF),
        ],
        name="ffn_weights_here",
        **kernel_params(4),
    )(place, w_up, w_down.reshape(LAYERS, 2, half, model), far)
    return up, down.reshape(hidden_local, model)


def ffn_grads_kernel(place_ref, mine_ref, other_ref, *refs):
    up_ref, down_ref = refs[-2:]
    slab, half = up_ref.shape[1], up_ref.shape[2] // 2
    for low in range(2):

        @pl.when(place_ref[0] == low)
        def _(pair=(mine_ref, other_ref) if low == 0 else (other_ref, mine_ref)):
            for n, piece in enumerate(pair):
                up_ref[0, :, n * half : (n + 1) * half] = piece[0, :slab].astype(F32)
                down_ref[0, n] = piece[0, slab:].astype(F32)


def ffn_grads(depth, place, mine, other, hidden_local, stacks=None):
    half = hidden_local // 2
    count, _, model = mine.shape
    slab, rows = model // count, half // count
    span = slab + rows
    shapes = [(LAYERS, model, hidden_local), (LAYERS, 2, half, model)]
    held = [] if stacks is None else list(stacks)
    return pl.pallas_call(
        ffn_grads_kernel,
        grid_spec=pltpu.PrefetchScalarGridSpec(
            num_scalar_prefetch=1,
            grid=(count,),
            in_specs=[pl.BlockSpec((1, span, model), lambda j, p: (j, 0, 0))] * 2
            + [pl.BlockSpec(memory_space=pl.ANY)] * len(held),
            out_specs=[
                pl.BlockSpec((1, slab, hidden_local), lambda j, p: (depth, j, 0)),
                pl.BlockSpec((1, 2, rows, model), lambda j, p: (depth, 0, j, 0)),
            ],
        ),
        out_shape=[jax.ShapeDtypeStruct(shape, F32) for shape in shapes],
        input_output_aliases={3 + n: n for n in range(len(held))},
        name="ffn_grads",
        **kernel_params(4),
    )(place, mine, other, *held)


def dot_nt(left, right, **options):
    return lax.dot_general(
        left, right, (((1,), (1,)), ((), ())), preferred_element_type=F32, **options
    )


def attend_forward_kernel(
    heads,
    own_x_ref,
    core_x_ref,
    plane_x_ref,
    both_x_ref,
    mix_w_ref,
    bias_ref,
    out_w_ref,
    own_ref,
    core_ref,
    plane_ref,
    both_ref,
    x_ref,
    mix_ref,
    o_ref,
    lse_ref,
    q_scr,
    k_scr,
    vt_scr,
    e_scr,
    ot_scr,
):
    blk = bias_ref.shape[1]
    width = heads * HD
    step = pl.program_id(0)

    @pl.when(step == 0)
    def _():
        for n, ref in enumerate((own_x_ref, core_x_ref, plane_x_ref, both_x_ref)):
            rows = slice(n * (blk // 2), (n + 1) * (blk // 2))
            mix = dot_nt(ref[...], mix_w_ref[...]).astype(BF)
            x_ref[rows, :] = ref[...]
            mix_ref[rows, :] = mix
            q_scr[rows, :] = mix[:, :width]
            k_scr[rows, :] = mix[:, width : 2 * width]
            vt_scr[:, rows] = mix[:, 2 * width :].T

    q = q_scr[pl.ds(pl.multiple_of(step * blk, blk), blk), :]
    head_of = lax.broadcasted_iota(jnp.int32, q.shape, 1) // HD
    totals = []
    for h in range(heads):
        q_head = jnp.where(head_of == h, q, jnp.zeros_like(q))
        scores = dot_nt(k_scr[...], q_head) * (LOG2_E / math.sqrt(HD)) + bias_ref[...]
        top = jnp.max(scores, axis=0, keepdims=True)
        expo = jnp.exp2(scores - top)
        total = jnp.sum(expo, axis=0, keepdims=True)
        totals.append(total)
        e_scr[:, h * blk : (h + 1) * blk] = expo.astype(BF)
        lse_ref[h : h + 1, :] = top + jnp.log2(total)
    wide = dot(vt_scr[...], e_scr[...])
    for h in range(heads):
        ot_scr[h * HD : (h + 1) * HD, :] = (
            wide[h * HD : (h + 1) * HD, h * blk : (h + 1) * blk] / totals[h]
        )
    o = ot_scr[...].T
    o_ref[...] = o
    part = dot(o.astype(BF), out_w_ref[...]).astype(BF)

    @pl.when(step == 0)
    def _():
        own_ref[...] = part[: blk // 2]
        core_ref[...] = part[blk // 2 :]

    @pl.when(step == 1)
    def _():
        plane_ref[...] = part[: blk // 2]
        both_ref[...] = part[blk // 2 :]


def attend_forward(blocks, mix_w, bias, out_w):
    part_rows, model = blocks[0].shape
    blk, rows = 2 * part_rows, 4 * part_rows
    width3 = mix_w.shape[0]
    width = out_w.shape[0]
    heads = width // HD
    return pl.pallas_call(
        functools.partial(attend_forward_kernel, heads),
        grid=(2,),
        in_specs=[whole(part_rows, model)] * 4
        + [
            whole(width3, model),
            pl.BlockSpec((rows, blk), lambda i: (0, i)),
            whole(width, model),
        ],
        out_specs=[whole(part_rows, model)] * 4
        + [
            whole(rows, model),
            whole(rows, width3),
            pl.BlockSpec((blk, width), lambda i: (i, 0)),
            pl.BlockSpec((8, blk), lambda i: (0, i)),
        ],
        out_shape=[jax.ShapeDtypeStruct((part_rows, model), BF)] * 4
        + [
            jax.ShapeDtypeStruct((rows, model), BF),
            jax.ShapeDtypeStruct((rows, width3), BF),
            jax.ShapeDtypeStruct((rows, width), F32),
            jax.ShapeDtypeStruct((8, rows), F32),
        ],
        scratch_shapes=[
            pltpu.VMEM((rows, width), BF),
            pltpu.VMEM((rows, width), BF),
            pltpu.VMEM((width, rows), BF),
            pltpu.VMEM((rows, heads * blk), BF),
            pltpu.VMEM((width, blk), F32),
        ],
        name="attend_forward",
        **kernel_params(4),
    )(*blocks, mix_w, bias, out_w)


def attend_backward_kernel(
    heads,
    mix_ref,
    bias_ref,
    mix_w_ref,
    out_w_ref,
    row_refs,
    o_ref,
    lse_ref,
    part_refs,
    grad_ref,
    grad_out_ref,
    q_scr,
    k_scr,
    kt_scr,
    v_scr,
    do_scr,
    p_scr,
    ds_scr,
    qh_scr,
    doh_scr,
    dqt_scr,
    dk_scr,
    dv_scr,
):
    blk = bias_ref.shape[1]
    width = heads * HD
    step = pl.program_id(0)
    scale = 1.0 / math.sqrt(HD)

    @pl.when(step == 0)
    def _():
        q_scr[...] = mix_ref[:, :width]
        k_scr[...] = mix_ref[:, width : 2 * width]
        v_scr[...] = mix_ref[:, 2 * width :]
        kt_scr[...] = k_scr[...].T
        dk_scr[...] = jnp.zeros_like(dk_scr)
        dv_scr[...] = jnp.zeros_like(dv_scr)
        grad_out = jnp.zeros(grad_out_ref.shape, F32)
        for n, ref in enumerate(row_refs):
            rows = slice(n * blk, (n + 1) * blk)
            do_scr[rows, :] = dot_nt(ref[...], out_w_ref[...]).astype(BF)
            grad_out = grad_out + dot(o_ref[rows, :].astype(BF).T, ref[...])
        grad_out_ref[...] = grad_out

    rows = pl.ds(pl.multiple_of(step * blk, blk), blk)
    q = q_scr[rows, :]
    do = do_scr[rows, :]
    head_of = lax.broadcasted_iota(jnp.int32, q.shape, 1) // HD
    pick = (
        lax.broadcasted_iota(jnp.int32, (8, width), 1) // HD
        == lax.broadcasted_iota(jnp.int32, (8, width), 0)
    ).astype(F32)
    inner = dot_nt(pick, do.astype(F32) * o_ref[rows, :], precision=lax.Precision.HIGHEST)
    for h in range(heads):
        cols = slice(h * blk, (h + 1) * blk)
        q_head = jnp.where(head_of == h, q, jnp.zeros_like(q))
        do_head = jnp.where(head_of == h, do, jnp.zeros_like(do))
        qh_scr[cols, :] = q_head
        doh_scr[cols, :] = do_head
        scores = dot_nt(k_scr[...], q_head) * (LOG2_E * scale) + bias_ref[...]
        probs = jnp.exp2(scores - lse_ref[h : h + 1, :])
        p_scr[:, cols] = probs.astype(BF)
        ds = (probs * (dot_nt(v_scr[...], do_head) - inner[h : h + 1, :])).astype(BF)
        ds_scr[:, cols] = ds
        dqt_scr[h * HD : (h + 1) * HD, :] = dot(kt_scr[h * HD : (h + 1) * HD, :], ds) * scale
    dv_scr[...] += dot(p_scr[...], doh_scr[...])
    dk_scr[...] += dot(ds_scr[...], qh_scr[...])
    grad_ref[rows, :width] = dqt_scr[...].T.astype(BF)

    @pl.when(step == pl.num_programs(0) - 1)
    def _():
        grad_ref[:, width : 2 * width] = (dk_scr[...] * scale).astype(BF)
        grad_ref[:, 2 * width :] = dv_scr[...].astype(BF)
        for n, ref in enumerate(part_refs):
            ref[...] = dot(grad_ref[n * blk : (n + 1) * blk, :], mix_w_ref[...]).astype(BF)


def attend_backward(mix, bias, mix_w, out_w, rows_four, o, lse):
    rows, width3 = mix.shape
    blk = rows // 4
    width, model = out_w.shape
    heads = width // HD

    def kernel(*refs):
        attend_backward_kernel(
            heads, *refs[:4], refs[4:8], *refs[8:10], refs[10:14], *refs[14:]
        )

    return pl.pallas_call(
        kernel,
        grid=(4,),
        in_specs=[
            whole(rows, width3),
            pl.BlockSpec((rows, blk), lambda i: (0, i)),
            whole(width3, model),
            whole(width, model),
        ]
        + [whole(blk, model)] * 4
        + [whole(rows, width), pl.BlockSpec((8, blk), lambda i: (0, i))],
        out_specs=[whole(blk, model)] * 4 + [whole(rows, width3), whole(width, model)],
        out_shape=[jax.ShapeDtypeStruct((blk, model), BF)] * 4
        + [
            jax.ShapeDtypeStruct((rows, width3), BF),
            jax.ShapeDtypeStruct((width, model), F32),
        ],
        scratch_shapes=[
            pltpu.VMEM((rows, width), BF),
            pltpu.VMEM((rows, width), BF),
            pltpu.VMEM((width, rows), BF),
            pltpu.VMEM((rows, width), BF),
            pltpu.VMEM((rows, width), BF),
            pltpu.VMEM((rows, heads * blk), BF),
            pltpu.VMEM((rows, heads * blk), BF),
            pltpu.VMEM((heads * blk, width), BF),
            pltpu.VMEM((heads * blk, width), BF),
            pltpu.VMEM((width, blk), F32),
            pltpu.VMEM((rows, width), F32),
            pltpu.VMEM((rows, width), F32),
        ],
        name="attend_backward",
        **kernel_params(6),
    )(mix, bias, mix_w, out_w, *rows_four, o, lse)


def local(
    tokens,
    lengths,
    key_keep,
    ln_gain,
    ln_bias,
    w_qkv,
    w_out,
    w_up,
    w_down,
    readout,
    labels,
    cotangent,
    *,
    rest,
):
    rows_shard, model_width = tokens.shape
    seq_len = key_keep.shape[1]
    local_width = w_qkv.shape[3]
    hidden_local = w_up.shape[2]
    half = hidden_local // 2
    r = lax.axis_index("r")
    c = lax.axis_index("c")
    zh = lax.axis_index("zh")
    zl = lax.axis_index("zl")
    at_home = c == zh
    slab = model_width // rest
    slab_half = half // rest
    slab_attn = 4 * local_width // rest
    span = slab + slab_half

    hidden = rehome(tokens)
    mix_weights = jnp.transpose(w_qkv, (0, 2, 3, 1)).reshape(LAYERS, 3 * local_width, model_width)
    mix_first = rehome(mix_weights[0])
    out_first = rehome(w_out[0])
    place = c.astype(jnp.int32)[None]
    tiled = slab % 16 == 0 and slab_half % 16 == 0

    def far_ffn(depth):
        parts = [
            lax.dynamic_slice(w_up[depth], (r * slab, c * half), (slab, half)),
            lax.dynamic_slice(w_down[depth], (c * half + r * slab_half, 0), (slab_half, model_width)),
        ]
        return jnp.concatenate(parts, axis=0)

    def far_attn(depth):
        both = jnp.concatenate([mix_weights[depth], w_out[depth]], axis=0)
        return lax.dynamic_slice(both, (r * slab_attn, 0), (slab_attn, model_width))

    def ffn_weights(depth, far):
        if tiled:
            return ffn_weights_here(depth, place, w_up, w_down, far)
        up_home = lax.dynamic_slice(w_up[depth], (0, c * half), (model_width, half))
        up_far = far[:, :slab].reshape(model_width, half)
        down_home = lax.dynamic_slice(w_down[depth], (c * half, 0), (half, model_width))
        down_far = far[:, slab:].reshape(half, model_width)
        return (
            jnp.concatenate([up_home, up_far], axis=1),
            jnp.concatenate([down_home, down_far], axis=0),
        )

    def attn_weights(depth, far):
        far = far.reshape(4 * local_width, model_width)
        return (
            jnp.where(at_home, mix_weights[depth], far[: 3 * local_width]),
            jnp.where(at_home, w_out[depth], far[3 * local_width :]),
        )

    col_ids = jnp.arange(seq_len, dtype=jnp.int32)
    allowed = ((col_ids[None, :] < lengths[:, None]) & (key_keep == 1)).astype(jnp.int32)
    allowed = jnp.where(at_home, allowed, flip(allowed, "c")).reshape(2, 2, rows_shard)
    allowed = jnp.where(c == 1, allowed[::-1], allowed)
    allowed = jnp.where(zl == 1, allowed[:, ::-1], allowed)
    allowed = jnp.swapaxes(allowed, 0, 1).reshape(seq_len) == 1
    bias = jnp.where(allowed[:, None] | (col_ids[:, None] == col_ids[None, :]), 0.0, NEG)

    hidden = tie(hidden, bias)
    parts = ()
    saved = []
    for depth in range(LAYERS):
        first, last = depth == 0, depth == LAYERS - 1
        hidden, normed = norm_forward(hidden, parts, ln_gain[depth, 0], ln_bias[depth, 0])
        attn_blocks = gather_start(normed)
        if first:
            mix_w, out_w = mix_first, out_first
        else:
            mix_w, out_w = attn_weights(1, tie(attn_1, normed))
        if first:
            shadow = far_0 = flip(tie(far_ffn(0), normed), "zh")
        else:
            far_1 = flip(tie(far_ffn(1), normed), "zh")
            down_blocks = gather_start(tie(cotangent_home, normed))
            shadow = far_1, down_blocks
        *attn_parts, x, mixed, attended, log_totals = tie(
            attend_forward(attn_blocks, mix_w, bias, out_w), shadow
        )
        sent, came = scatter_far(*attn_parts[2:])
        attn_parts = (attn_parts[0], flip(attn_parts[1], "c"), came)
        if first:
            far_0 = spread_rest(tie(far_0, sent), rest)
            attn_1 = flip(tie(far_attn(1), sent), "zh")
            cotangent_home = rehome(tie(cotangent, attn_parts[2]))
        else:
            far_1 = spread_rest(tie(far_1, sent), rest)
        middle, normed_two = norm_forward(
            hidden, attn_parts, ln_gain[depth, 1], ln_bias[depth, 1]
        )
        ffn_blocks = gather_start(normed_two)
        if first:
            up_w, down_w = ffn_weights(depth, tie(far_0, normed_two))
        else:
            up_w, down_w = ffn_weights(depth, tie(far_1, normed_two))
        ffn_outs, acts, us = zip(*(ffn_forward(b, up_w, down_w) for b in ffn_blocks))
        own, core, plane, both = ffn_outs
        if first:
            plane, both = tie((plane, both), attn_1, cotangent_home)
            attn_1 = spread_rest(attn_1, rest)
            sent, came = scatter_far(plane, both)
            parts = (own, flip(core, "c"), came)
        saved.append(
            dict(
                entry=hidden,
                middle=middle,
                x=x,
                mixed=mixed,
                attended=attended,
                log_totals=log_totals,
                ffn=ffn_blocks,
                act=acts,
                u=us,
                weights=(mix_w, out_w, up_w, down_w),
            )
        )
        hidden = middle
    last_parts = (own, core, plane, both)

    def transposed_dot(left, right):
        left, right = (jnp.concatenate(x, axis=0) for x in (left, right))
        return dot(left.T, right).astype(BF)

    def ffn_blocks_backward(keep, blocks, before=()):
        _, _, up_w, down_w = keep["weights"]
        outs, pres = [None] * 4, [None] * 4
        for k in (3, 2):
            outs[k], pres[k] = ffn_backward(blocks[k], up_w, down_w, keep["u"][k])
        sent, came = scatter_far(*tie(outs[2:], before))
        for k in (1, 0):
            outs[k], pres[k] = ffn_backward(blocks[k], up_w, down_w, keep["u"][k])
        parts = (outs[0], flip(outs[1], "c"), came)
        grad_down = transposed_dot(tie(keep["act"], sent), blocks)
        grad_up = transposed_dot(tie(keep["ffn"], sent), pres)
        return parts, sent, ffn_grad_rows(grad_up, grad_down)

    def ffn_grad_rows(grad_up, grad_down):
        rows = [
            grad_up[:, :half].reshape(rest, slab, half),
            grad_down[:half].reshape(rest, slab_half, model_width),
            grad_up[:, half:].reshape(rest, slab, half),
            grad_down[half:].reshape(rest, slab_half, model_width),
        ]
        return jnp.concatenate(rows, axis=1)

    def finish_ffn(depth, mine, other, stacks):
        if tiled:
            return ffn_grads(depth, place, mine, other, hidden_local, stacks)
        low, high = (jnp.where(c == k, mine, other) for k in (0, 1))
        up = jnp.concatenate([x[:, :slab].reshape(model_width, half) for x in (low, high)], axis=1)
        down = jnp.stack([x[:, slab:span].reshape(half, model_width) for x in (low, high)])
        new = (up.astype(F32), down.astype(F32))
        if stacks is None:
            return [jnp.stack([x] * LAYERS) for x in new]
        return [x.at[depth].set(y) for x, y in zip(stacks, new)]

    def attn_grad_rows(grad_mix, grad_out):
        rows = jnp.concatenate([grad_mix.astype(BF), grad_out.astype(BF)], axis=0)
        return rows.reshape(rest, slab_attn, model_width)

    def finish_attn(mine, other):
        sums = jnp.where(
            at_home, mine[:, span : span + slab_attn], other[:, span : span + slab_attn]
        )
        sums = sums.reshape(4 * local_width, model_width)
        mix = sums[: 3 * local_width].reshape(3, local_width, model_width)
        return mix.astype(F32), sums[3 * local_width :].astype(F32)

    def added(one, two):
        return (one.astype(F32) + two.astype(F32)).astype(BF)

    def attn_backward(keep, row_blocks):
        mix_w, out_w, _, _ = keep["weights"]
        return attend_backward(
            keep["mixed"], bias, mix_w, out_w, row_blocks, keep["attended"], keep["log_totals"]
        )

    def sum_first(x):
        return jnp.sum(x.astype(F32), axis=0)

    keep = saved[1]
    parts, sent, ffn_a = ffn_blocks_backward(keep, down_blocks)
    ffn_a = exchange_rest(ffn_a)
    grad, low, sums_11 = norm_backward(parts, keep["middle"], cotangent_home, ln_gain[1, 1])
    row_blocks = gather_start(low)

    own, core, plane, both = tie(last_parts, row_blocks)
    _, plane = scatter_far(plane, both)
    core = flip(core, "c")
    *parts, mix_grad, grad_out = tie(attn_backward(keep, row_blocks), plane, core, ffn_a)
    sent, came = scatter_far(*parts[2:])
    parts = (parts[0], flip(parts[1], "c"), came)
    ffn_a = sum_first(tie(ffn_a, sent)).astype(BF)
    grad_mix = dot(tie(mix_grad, sent).T, keep["x"])
    attn_a = attn_grad_rows(grad_mix, grad_out)
    grad, low, sums_10 = norm_backward(parts, keep["entry"], grad, ln_gain[1, 0])
    attn_a = exchange_rest(attn_a)

    down_blocks = gather_start(low)
    keep = saved[0]
    parts, sent, ffn_b = ffn_blocks_backward(keep, down_blocks)
    attn_a = sum_first(tie(attn_a, sent)).astype(BF)
    parts, ffn_b = tie((parts, ffn_b), attn_a)
    ffn_b = exchange_rest(ffn_b)
    grad, low, sums_01 = norm_backward(parts, keep["middle"], grad, ln_gain[0, 1])
    row_blocks = gather_start(low)
    plane, core = tie((plane, core), low)
    final = saved[1]["middle"] + own.astype(F32) + core.astype(F32) + plane.astype(F32)
    held = jnp.concatenate([ffn_a[span:], attn_a], axis=0)
    came_a = flip(tie(held, low), "zh")

    *parts, mix_grad, grad_out = tie(attn_backward(keep, row_blocks), ffn_b, came_a)
    sent, came = scatter_far(*parts[2:])
    parts = (parts[0], flip(parts[1], "c"), came)
    ffn_b = sum_first(tie(ffn_b, sent))
    came_b = flip(ffn_b[span:].astype(BF), "zh")
    grad_mix = dot(tie(mix_grad, sent).T, keep["x"])
    attn_b = exchange_rest(attn_grad_rows(grad_mix, grad_out))
    grad, low, sums_00 = norm_backward(parts, keep["entry"], grad, ln_gain[0, 0])

    first_of_four = (zh == 0) & (zl == 0)
    count = jnp.where(first_of_four, lengths[0], 0).astype(F32)
    sums = jnp.stack([sums_00, sums_01, sums_10, sums_11])
    small = jnp.concatenate(
        [
            sums[:, 0],
            sums[:, 1],
            jnp.broadcast_to(count, (1, model_width)),
            jnp.zeros((16 - 4 * LAYERS - 1, model_width), F32),
        ],
        axis=0,
    )
    small = small + flip(small, "zl")

    def in_two(x):
        high = lax.reduce_precision(x, 8, 7)
        return jnp.concatenate([high, x - high], axis=0).astype(BF)

    def from_two(x):
        high, rest_of_it = jnp.split(x.astype(F32), 2, axis=-2)
        return high + rest_of_it

    attn_b = sum_first(tie(attn_b, low)).astype(BF)
    sent_c = jnp.concatenate([attn_b, in_two(small)], axis=0)
    came_c = flip(sent_c, "zh")
    small = small + from_two(came_c[slab_attn:])
    rows_b = jnp.concatenate(
        [
            (ffn_b[:span] + came_b.astype(F32)).astype(BF),
            added(attn_b, came_c[:slab_attn]),
            in_two(small),
        ],
        axis=0,
    )
    rows_b = spread_rest(rows_b, rest)
    layer_out = rehome(tie(final.astype(BF), low))
    grad_tokens = rehome(low)
    row_ids = (2 * zh + zl) * rows_shard + jnp.arange(rows_shard, dtype=jnp.int32)
    live_rows = row_ids < lengths[0]
    logits = dot(layer_out, readout)
    top = jnp.max(logits, axis=-1, keepdims=True)
    log_total = top[:, 0] + jnp.log(jnp.sum(jnp.exp(logits - top), axis=-1))
    classes = jnp.arange(logits.shape[1], dtype=jnp.int32)
    picked = jnp.sum(jnp.where(labels[:, None] == classes[None, :], logits, 0.0), axis=-1)
    label_logprob = jnp.where(live_rows, picked - log_total, jnp.zeros_like(log_total))

    rows_a = added(jnp.concatenate([ffn_a[:span], attn_a], axis=0), came_a)
    rows_a = spread_rest(tie(rows_a, rows_b), rest)
    rows_b, layer_out, label_logprob, grad_tokens = tie(
        (rows_b, layer_out, label_logprob, grad_tokens)
    )
    rows_b = (rows_b, flip(rows_b, "c"))
    ffn_stacks = finish_ffn(0, *rows_b, None)
    attn_b = finish_attn(*rows_b)
    small = sum(jnp.sum(from_two(x[:, span + slab_attn :]), axis=0) for x in rows_b)
    rows_a, ffn_stacks, attn_b, small = tie((rows_a, ffn_stacks, attn_b, small))
    rows_a = (rows_a, flip(rows_a, "c"))
    grads_up, grads_down = finish_ffn(1, *rows_a, ffn_stacks)
    attn_a = finish_attn(*rows_a)
    grads_mix, grads_out = (jnp.stack(pair) for pair in zip(attn_b, attn_a))
    grads_mix = jnp.transpose(grads_mix, (0, 3, 1, 2))
    grad_tokens = grad_tokens.astype(F32)
    gain_total = small[: 2 * LAYERS].reshape(LAYERS, 2, model_width)
    shift_total = small[2 * LAYERS : 4 * LAYERS].reshape(LAYERS, 2, model_width)
    token_count = small[4 * LAYERS, 0].astype(jnp.int32)
    return (
        layer_out,
        grad_tokens,
        gain_total,
        shift_total,
        grads_mix,
        grads_out,
        grads_up,
        grads_down.reshape(LAYERS, hidden_local, model_width),
        label_logprob,
        token_count,
    )


def solution(mesh):
    batch, model = mesh.devices.shape
    rest = batch // 2
    fine = Mesh(mesh.devices.reshape(rest, 2, 2, model // 2), ("r", "c", "zh", "zl"))
    dp = ("r", "c")
    mp = ("zh", "zl")
    both = dp + mp
    in_specs = (
        P(both, None),
        P(dp),
        P(dp, None),
        P(),
        P(),
        P(None, None, None, mp),
        P(None, mp, None),
        P(None, None, mp),
        P(None, mp, None),
        P(),
        P(both),
        P(both, None),
    )
    out_specs = (
        P(both, None),
        P(both, None),
        P(),
        P(),
        P(None, None, None, mp),
        P(None, mp, None),
        P(None, None, mp),
        P(None, mp, None),
        P(both),
        P(),
    )

    def body(*args):
        return local(*args, rest=rest)

    return jax.shard_map(body, mesh=fine, in_specs=in_specs, out_specs=out_specs, check_vma=False)
```

```python
import functools
import math

import jax
import jax.numpy as jnp
from jax import lax
from jax.experimental import pallas as pl
from jax.experimental.pallas import tpu as pltpu
from jax.sharding import Mesh, PartitionSpec as P

HD = 32
LAYERS = 2


EPS = 1e-05
NEG = -1000000000.0
ROOT_HALF = 0.7071067811865476
INV_ROOT_TAU = 0.3989422804014327
LOG2_E = 1.4426950408889634
VMEM_LIMIT = 56 * 1024 * 1024

BF = jnp.bfloat16
F32 = jnp.float32
FLIP = [(0, 1), (1, 0)]

HOME = []
for _c in range(2):
    for _h in range(2):
        for _p in range(2):
            _to = (_c, _h, _p) if _c == _h else (1 - _c, 1 - _h, _p)
            HOME.append((4 * _c + 2 * _h + _p, 4 * _to[0] + 2 * _to[1] + _to[2]))


def rehome(x):
    return lax.ppermute(x, ("c", "zh", "zl"), HOME)


def flip(x, axis):
    return lax.ppermute(x, axis, FLIP)


def tie(x, *before):
    return lax.optimization_barrier((x, before))[0]


def whole(*shape):
    return pl.BlockSpec(shape, lambda *_: (0,) * len(shape))


def kernel_params(micros):
    return dict(
        compiler_params=pltpu.CompilerParams(vmem_limit_bytes=VMEM_LIMIT),
        cost_estimate=pl.CostEstimate(
            flops=int(micros * 1.15e9), bytes_accessed=1 << 20, transcendentals=0
        ),
    )


def norm_unit(values):
    mean = jnp.mean(values, axis=-1, keepdims=True)
    centred = values - mean
    spread = jnp.mean(centred * centred, axis=-1, keepdims=True)
    inverse = lax.rsqrt(spread + EPS)
    return centred * inverse, inverse


def norm_forward_kernel(count, hidden_ref, *refs):
    parts = refs[:count]
    gain_ref, bias_ref, sum_ref, normed_ref = refs[count:]
    values = hidden_ref[...].astype(F32)
    for part in parts:
        values = values + part[...].astype(F32)
    sum_ref[...] = values
    unit, _ = norm_unit(values)
    normed_ref[...] = (unit * gain_ref[...] + bias_ref[...]).astype(BF)


def norm_forward(hidden, parts, gain, bias):
    rows, model = hidden.shape
    return pl.pallas_call(
        functools.partial(norm_forward_kernel, len(parts)),
        out_shape=[
            jax.ShapeDtypeStruct((rows, model), F32),
            jax.ShapeDtypeStruct((rows, model), BF),
        ],
        name="norm_forward",
        **kernel_params(2.5),
    )(hidden, *parts, gain[None], bias[None])


def norm_backward_kernel(
    own_ref, core_ref, plane_ref, values_ref, grad_ref, gain_ref, out_ref, low_ref, sums_ref
):
    grad_normed = own_ref[...].astype(F32) + core_ref[...].astype(F32) + plane_ref[...].astype(F32)
    unit, inverse = norm_unit(values_ref[...])
    scaled = grad_normed * gain_ref[...]
    mean_one = jnp.mean(scaled, axis=-1, keepdims=True)
    mean_two = jnp.mean(scaled * unit, axis=-1, keepdims=True)
    grad = grad_ref[...].astype(F32) + inverse * (scaled - mean_one - unit * mean_two)
    out_ref[...] = grad
    low_ref[...] = grad.astype(BF)
    sums_ref[0:1, :] = jnp.sum(grad_normed * unit, axis=0, keepdims=True)
    sums_ref[1:2, :] = jnp.sum(grad_normed, axis=0, keepdims=True)


def norm_backward(parts, values, grad, gain):
    rows, model = values.shape
    return pl.pallas_call(
        norm_backward_kernel,
        out_shape=[
            jax.ShapeDtypeStruct((rows, model), F32),
            jax.ShapeDtypeStruct((rows, model), BF),
            jax.ShapeDtypeStruct((2, model), F32),
        ],
        name="norm_backward",
        **kernel_params(3),
    )(*parts, values, grad, gain[None])


def gelu_and_slope(u):
    cdf = 0.5 * (1.0 + lax.erf(u * ROOT_HALF))
    return (u * cdf).astype(BF), cdf + u * jnp.exp(-0.5 * u * u) * INV_ROOT_TAU


def ffn_forward(x, up_w, down_w):
    u = dot(x, up_w)
    act = gelu_and_slope(u)[0]
    return dot(act, down_w).astype(BF), act, u


def ffn_backward(x, up_w, down_w, u):
    grad = (dot_nt(x, down_w) * gelu_and_slope(u)[1]).astype(BF)
    return dot_nt(grad, up_w).astype(BF), grad


def dot(left, right):
    return jnp.dot(left, right, preferred_element_type=F32)


def gather_start(x):
    plane = flip(x, "zl")
    return x, flip(x, "c"), plane, flip(plane, "c")


def scatter_far(plane, both):
    both = flip(both, "c")
    sent = (plane.astype(F32) + both.astype(F32)).astype(BF)
    return sent, flip(sent, "zl")


def exchange_rest(x):
    return lax.all_to_all(x, "r", 0, 0)


def spread_rest(x, count):
    return exchange_rest(jnp.broadcast_to(x[None], (count,) + x.shape))


def permute_rest(x, count):
    if count != 4:
        return spread_rest(x, count)
    r = lax.axis_index("r")
    pieces = [x] + [lax.ppermute(x, "r", [(i, i ^ k) for i in range(count)]) for k in range(1, count)]
    pieces = jnp.stack(pieces)
    return jnp.stack([lax.dynamic_index_in_dim(pieces, r ^ k, keepdims=False) for k in range(count)])


def weights_kernel(place_ref, up_home_ref, down_home_ref, far_ref, up_ref, down_ref):
    slab, half = up_home_ref.shape[1:]
    up_ref[:, :half] = up_home_ref[0]
    up_ref[:, half:] = far_ref[0, :slab]
    down_ref[0] = down_home_ref[0, 0]
    down_ref[1] = far_ref[0, slab:]


def ffn_weights_here(depth, place, w_up, w_down, far):
    model, hidden_local = w_up.shape[1:]
    half = hidden_local // 2
    count, span = far.shape[:2]
    slab, rows = model // count, half // count
    up, down = pl.pallas_call(
        weights_kernel,
        grid_spec=pltpu.PrefetchScalarGridSpec(
            num_scalar_prefetch=1,
            grid=(count,),
            in_specs=[
                pl.BlockSpec((1, slab, half), lambda j, p: (depth, j, p[0])),
                pl.BlockSpec((1, 1, rows, model), lambda j, p: (depth, p[0], j, 0)),
                pl.BlockSpec((1, span, model), lambda j, p: (j, 0, 0)),
            ],
            out_specs=[
                pl.BlockSpec((slab, hidden_local), lambda j, p: (j, 0)),
                pl.BlockSpec((2, rows, model), lambda j, p: (0, j, 0)),
            ],
        ),
        out_shape=[
            jax.ShapeDtypeStruct((model, hidden_local), BF),
            jax.ShapeDtypeStruct((2, half, model), BF),
        ],
        name="ffn_weights_here",
        **kernel_params(4),
    )(place, w_up, w_down.reshape(LAYERS, 2, half, model), far)
    return up, down.reshape(hidden_local, model)


def ffn_grads_kernel(place_ref, mine_ref, other_ref, *refs):
    up_ref, down_ref = refs[-2:]
    slab, half = up_ref.shape[1], up_ref.shape[2] // 2
    for low in range(2):

        @pl.when(place_ref[0] == low)
        def _(pair=(mine_ref, other_ref) if low == 0 else (other_ref, mine_ref)):
            for n, piece in enumerate(pair):
                up_ref[0, :, n * half : (n + 1) * half] = piece[0, :slab].astype(F32)
                down_ref[0, n] = piece[0, slab:].astype(F32)


def ffn_grads(depth, place, mine, other, hidden_local, stacks=None):
    half = hidden_local // 2
    count, _, model = mine.shape
    slab, rows = model // count, half // count
    span = slab + rows
    shapes = [(LAYERS, model, hidden_local), (LAYERS, 2, half, model)]
    held = [] if stacks is None else list(stacks)
    return pl.pallas_call(
        ffn_grads_kernel,
        grid_spec=pltpu.PrefetchScalarGridSpec(
            num_scalar_prefetch=1,
            grid=(count,),
            in_specs=[pl.BlockSpec((1, span, model), lambda j, p: (j, 0, 0))] * 2
            + [pl.BlockSpec(memory_space=pl.ANY)] * len(held),
            out_specs=[
                pl.BlockSpec((1, slab, hidden_local), lambda j, p: (depth, j, 0)),
                pl.BlockSpec((1, 2, rows, model), lambda j, p: (depth, 0, j, 0)),
            ],
        ),
        out_shape=[jax.ShapeDtypeStruct(shape, F32) for shape in shapes],
        input_output_aliases={3 + n: n for n in range(len(held))},
        name="ffn_grads",
        **kernel_params(4),
    )(place, mine, other, *held)


def dot_nt(left, right, **options):
    return lax.dot_general(
        left, right, (((1,), (1,)), ((), ())), preferred_element_type=F32, **options
    )


def attend_forward_kernel(
    heads,
    own_x_ref,
    core_x_ref,
    plane_x_ref,
    both_x_ref,
    mix_w_ref,
    bias_ref,
    out_w_ref,
    own_ref,
    core_ref,
    plane_ref,
    both_ref,
    x_ref,
    mix_ref,
    o_ref,
    lse_ref,
    q_scr,
    k_scr,
    vt_scr,
    e_scr,
    ot_scr,
):
    blk = bias_ref.shape[1]
    width = heads * HD
    step = pl.program_id(0)

    @pl.when(step == 0)
    def _():
        for n, ref in enumerate((own_x_ref, core_x_ref, plane_x_ref, both_x_ref)):
            rows = slice(n * (blk // 2), (n + 1) * (blk // 2))
            mix = dot_nt(ref[...], mix_w_ref[...]).astype(BF)
            x_ref[rows, :] = ref[...]
            mix_ref[rows, :] = mix
            q_scr[rows, :] = mix[:, :width]
            k_scr[rows, :] = mix[:, width : 2 * width]
            vt_scr[:, rows] = mix[:, 2 * width :].T

    q = q_scr[pl.ds(pl.multiple_of(step * blk, blk), blk), :]
    head_of = lax.broadcasted_iota(jnp.int32, q.shape, 1) // HD
    totals = []
    for h in range(heads):
        q_head = jnp.where(head_of == h, q, jnp.zeros_like(q))
        scores = dot_nt(k_scr[...], q_head) * (LOG2_E / math.sqrt(HD)) + bias_ref[...]
        top = jnp.max(scores, axis=0, keepdims=True)
        expo = jnp.exp2(scores - top)
        total = jnp.sum(expo, axis=0, keepdims=True)
        totals.append(total)
        e_scr[:, h * blk : (h + 1) * blk] = expo.astype(BF)
        lse_ref[h : h + 1, :] = top + jnp.log2(total)
    wide = dot(vt_scr[...], e_scr[...])
    for h in range(heads):
        ot_scr[h * HD : (h + 1) * HD, :] = (
            wide[h * HD : (h + 1) * HD, h * blk : (h + 1) * blk] / totals[h]
        )
    o = ot_scr[...].T
    o_ref[...] = o
    part = dot(o.astype(BF), out_w_ref[...]).astype(BF)

    @pl.when(step == 0)
    def _():
        own_ref[...] = part[: blk // 2]
        core_ref[...] = part[blk // 2 :]

    @pl.when(step == 1)
    def _():
        plane_ref[...] = part[: blk // 2]
        both_ref[...] = part[blk // 2 :]


def attend_forward(blocks, mix_w, bias, out_w):
    part_rows, model = blocks[0].shape
    blk, rows = 2 * part_rows, 4 * part_rows
    width3 = mix_w.shape[0]
    width = out_w.shape[0]
    heads = width // HD
    return pl.pallas_call(
        functools.partial(attend_forward_kernel, heads),
        grid=(2,),
        in_specs=[whole(part_rows, model)] * 4
        + [
            whole(width3, model),
            pl.BlockSpec((rows, blk), lambda i: (0, i)),
            whole(width, model),
        ],
        out_specs=[whole(part_rows, model)] * 4
        + [
            whole(rows, model),
            whole(rows, width3),
            pl.BlockSpec((blk, width), lambda i: (i, 0)),
            pl.BlockSpec((8, blk), lambda i: (0, i)),
        ],
        out_shape=[jax.ShapeDtypeStruct((part_rows, model), BF)] * 4
        + [
            jax.ShapeDtypeStruct((rows, model), BF),
            jax.ShapeDtypeStruct((rows, width3), BF),
            jax.ShapeDtypeStruct((rows, width), F32),
            jax.ShapeDtypeStruct((8, rows), F32),
        ],
        scratch_shapes=[
            pltpu.VMEM((rows, width), BF),
            pltpu.VMEM((rows, width), BF),
            pltpu.VMEM((width, rows), BF),
            pltpu.VMEM((rows, heads * blk), BF),
            pltpu.VMEM((width, blk), F32),
        ],
        name="attend_forward",
        **kernel_params(4),
    )(*blocks, mix_w, bias, out_w)


def attend_backward_kernel(
    heads,
    mix_ref,
    bias_ref,
    mix_w_ref,
    out_w_ref,
    row_refs,
    o_ref,
    lse_ref,
    part_refs,
    grad_ref,
    grad_out_ref,
    q_scr,
    k_scr,
    kt_scr,
    v_scr,
    do_scr,
    p_scr,
    ds_scr,
    qh_scr,
    doh_scr,
    dqt_scr,
    dk_scr,
    dv_scr,
):
    blk = bias_ref.shape[1]
    width = heads * HD
    step = pl.program_id(0)
    scale = 1.0 / math.sqrt(HD)

    @pl.when(step == 0)
    def _():
        q_scr[...] = mix_ref[:, :width]
        k_scr[...] = mix_ref[:, width : 2 * width]
        v_scr[...] = mix_ref[:, 2 * width :]
        kt_scr[...] = k_scr[...].T
        dk_scr[...] = jnp.zeros_like(dk_scr)
        dv_scr[...] = jnp.zeros_like(dv_scr)
        grad_out = jnp.zeros(grad_out_ref.shape, F32)
        for n, ref in enumerate(row_refs):
            rows = slice(n * blk, (n + 1) * blk)
            do_scr[rows, :] = dot_nt(ref[...], out_w_ref[...]).astype(BF)
            grad_out = grad_out + dot(o_ref[rows, :].astype(BF).T, ref[...])
        grad_out_ref[...] = grad_out

    rows = pl.ds(pl.multiple_of(step * blk, blk), blk)
    q = q_scr[rows, :]
    do = do_scr[rows, :]
    head_of = lax.broadcasted_iota(jnp.int32, q.shape, 1) // HD
    pick = (
        lax.broadcasted_iota(jnp.int32, (8, width), 1) // HD
        == lax.broadcasted_iota(jnp.int32, (8, width), 0)
    ).astype(F32)
    inner = dot_nt(pick, do.astype(F32) * o_ref[rows, :], precision=lax.Precision.HIGHEST)
    for h in range(heads):
        cols = slice(h * blk, (h + 1) * blk)
        q_head = jnp.where(head_of == h, q, jnp.zeros_like(q))
        do_head = jnp.where(head_of == h, do, jnp.zeros_like(do))
        qh_scr[cols, :] = q_head
        doh_scr[cols, :] = do_head
        scores = dot_nt(k_scr[...], q_head) * (LOG2_E * scale) + bias_ref[...]
        probs = jnp.exp2(scores - lse_ref[h : h + 1, :])
        p_scr[:, cols] = probs.astype(BF)
        ds = (probs * (dot_nt(v_scr[...], do_head) - inner[h : h + 1, :])).astype(BF)
        ds_scr[:, cols] = ds
    wide = dot(kt_scr[...], ds_scr[...])
    for h in range(heads):
        dqt_scr[h * HD : (h + 1) * HD, :] = (
            wide[h * HD : (h + 1) * HD, h * blk : (h + 1) * blk] * scale
        )
    dv_scr[...] += dot(p_scr[...], doh_scr[...])
    dk_scr[...] += dot(ds_scr[...], qh_scr[...])
    grad_ref[rows, :width] = dqt_scr[...].T.astype(BF)

    @pl.when(step == pl.num_programs(0) - 1)
    def _():
        grad_ref[:, width : 2 * width] = (dk_scr[...] * scale).astype(BF)
        grad_ref[:, 2 * width :] = dv_scr[...].astype(BF)
        for n, ref in enumerate(part_refs):
            ref[...] = dot(grad_ref[n * blk : (n + 1) * blk, :], mix_w_ref[...]).astype(BF)


def attend_backward(mix, bias, mix_w, out_w, rows_four, o, lse):
    rows, width3 = mix.shape
    blk = rows // 4
    width, model = out_w.shape
    heads = width // HD

    def kernel(*refs):
        attend_backward_kernel(
            heads, *refs[:4], refs[4:8], *refs[8:10], refs[10:14], *refs[14:]
        )

    return pl.pallas_call(
        kernel,
        grid=(4,),
        in_specs=[
            whole(rows, width3),
            pl.BlockSpec((rows, blk), lambda i: (0, i)),
            whole(width3, model),
            whole(width, model),
        ]
        + [whole(blk, model)] * 4
        + [whole(rows, width), pl.BlockSpec((8, blk), lambda i: (0, i))],
        out_specs=[whole(blk, model)] * 4 + [whole(rows, width3), whole(width, model)],
        out_shape=[jax.ShapeDtypeStruct((blk, model), BF)] * 4
        + [
            jax.ShapeDtypeStruct((rows, width3), BF),
            jax.ShapeDtypeStruct((width, model), F32),
        ],
        scratch_shapes=[
            pltpu.VMEM((rows, width), BF),
            pltpu.VMEM((rows, width), BF),
            pltpu.VMEM((width, rows), BF),
            pltpu.VMEM((rows, width), BF),
            pltpu.VMEM((rows, width), BF),
            pltpu.VMEM((rows, heads * blk), BF),
            pltpu.VMEM((rows, heads * blk), BF),
            pltpu.VMEM((heads * blk, width), BF),
            pltpu.VMEM((heads * blk, width), BF),
            pltpu.VMEM((width, blk), F32),
            pltpu.VMEM((rows, width), F32),
            pltpu.VMEM((rows, width), F32),
        ],
        name="attend_backward",
        **kernel_params(6),
    )(mix, bias, mix_w, out_w, *rows_four, o, lse)


def local(
    tokens,
    lengths,
    key_keep,
    ln_gain,
    ln_bias,
    w_qkv,
    w_out,
    w_up,
    w_down,
    readout,
    labels,
    cotangent,
    *,
    rest,
):
    rows_shard, model_width = tokens.shape
    seq_len = key_keep.shape[1]
    local_width = w_qkv.shape[3]
    hidden_local = w_up.shape[2]
    half = hidden_local // 2
    r = lax.axis_index("r")
    c = lax.axis_index("c")
    zh = lax.axis_index("zh")
    zl = lax.axis_index("zl")
    at_home = c == zh
    slab = model_width // rest
    slab_half = half // rest
    slab_attn = 4 * local_width // rest
    span = slab + slab_half

    hidden = rehome(tokens)
    mix_weights = jnp.transpose(w_qkv, (0, 2, 3, 1)).reshape(LAYERS, 3 * local_width, model_width)
    mix_first = rehome(mix_weights[0])
    out_first = rehome(w_out[0])
    place = c.astype(jnp.int32)[None]
    tiled = slab % 16 == 0 and slab_half % 16 == 0

    def far_ffn(depth):
        parts = [
            lax.dynamic_slice(w_up[depth], (r * slab, c * half), (slab, half)),
            lax.dynamic_slice(w_down[depth], (c * half + r * slab_half, 0), (slab_half, model_width)),
        ]
        return jnp.concatenate(parts, axis=0)

    def far_attn(depth):
        both = jnp.concatenate([mix_weights[depth], w_out[depth]], axis=0)
        return lax.dynamic_slice(both, (r * slab_attn, 0), (slab_attn, model_width))

    def ffn_weights(depth, far):
        if tiled:
            return ffn_weights_here(depth, place, w_up, w_down, far)
        up_home = lax.dynamic_slice(w_up[depth], (0, c * half), (model_width, half))
        up_far = far[:, :slab].reshape(model_width, half)
        down_home = lax.dynamic_slice(w_down[depth], (c * half, 0), (half, model_width))
        down_far = far[:, slab:].reshape(half, model_width)
        return (
            jnp.concatenate([up_home, up_far], axis=1),
            jnp.concatenate([down_home, down_far], axis=0),
        )

    def attn_weights(depth, far):
        far = far.reshape(4 * local_width, model_width)
        return (
            jnp.where(at_home, mix_weights[depth], far[: 3 * local_width]),
            jnp.where(at_home, w_out[depth], far[3 * local_width :]),
        )

    col_ids = jnp.arange(seq_len, dtype=jnp.int32)
    allowed = ((col_ids[None, :] < lengths[:, None]) & (key_keep == 1)).astype(jnp.int32)
    allowed = jnp.where(at_home, allowed, flip(allowed, "c")).reshape(2, 2, rows_shard)
    allowed = jnp.where(c == 1, allowed[::-1], allowed)
    allowed = jnp.where(zl == 1, allowed[:, ::-1], allowed)
    allowed = jnp.swapaxes(allowed, 0, 1).reshape(seq_len) == 1
    bias = jnp.where(allowed[:, None] | (col_ids[:, None] == col_ids[None, :]), 0.0, NEG)

    hidden = tie(hidden, bias)
    parts = ()
    saved = []
    for depth in range(LAYERS):
        first, last = depth == 0, depth == LAYERS - 1
        hidden, normed = norm_forward(hidden, parts, ln_gain[depth, 0], ln_bias[depth, 0])
        attn_blocks = gather_start(normed)
        if first:
            mix_w, out_w = mix_first, out_first
        else:
            mix_w, out_w = attn_weights(1, tie(attn_1, normed))
        if first:
            far_0 = tie(far_ffn(0), normed)
            attn_blocks = tie(attn_blocks, far_0)
            shadow = far_0 = flip(far_0, "zh")
        else:
            shadow = far_1 = flip(tie(far_ffn(1), attn_blocks[2]), "zh")
        *attn_parts, x, mixed, attended, log_totals = tie(
            attend_forward(attn_blocks, mix_w, bias, out_w), shadow
        )
        sent, came = scatter_far(*attn_parts[2:])
        attn_parts = (attn_parts[0], flip(attn_parts[1], "c"), came)
        if first:
            far_0 = spread_rest(tie(far_0, sent), rest)
            attn_1 = flip(tie(far_attn(1), sent), "zh")
            cotangent_home = rehome(tie(cotangent, attn_parts[2]))
        else:
            far_1 = spread_rest(tie(far_1, sent), rest)
        middle, normed_two = norm_forward(
            hidden, attn_parts, ln_gain[depth, 1], ln_bias[depth, 1]
        )
        ffn_blocks = gather_start(normed_two)
        if first:
            up_w, down_w = ffn_weights(depth, tie(far_0, normed_two))
        else:
            up_w, down_w = ffn_weights(depth, tie(far_1, normed_two))
        ffn_blocks = tie(ffn_blocks, up_w, down_w)
        if last:
            down_blocks = gather_start(tie(cotangent_home, ffn_blocks[2]))
        ffn_outs, acts, us = zip(*(ffn_forward(b, up_w, down_w) for b in ffn_blocks))
        own, core, plane, both = ffn_outs
        if first:
            plane, both = tie((plane, both), attn_1, cotangent_home)
            sent, came = scatter_far(plane, both)
            attn_1 = spread_rest(tie(attn_1, sent), rest)
            parts = (own, flip(core, "c"), came)
        saved.append(
            dict(
                entry=hidden,
                middle=middle,
                x=x,
                mixed=mixed,
                attended=attended,
                log_totals=log_totals,
                ffn=ffn_blocks,
                act=acts,
                u=us,
                weights=(mix_w, out_w, up_w, down_w),
            )
        )
        hidden = middle
    last_parts = (own, core, plane, both)

    def transposed_dot(left, right):
        left, right = (jnp.concatenate(x, axis=0) for x in (left, right))
        return dot(left.T, right).astype(BF)

    def ffn_blocks_backward(keep, blocks):
        _, _, up_w, down_w = keep["weights"]
        outs, pres = [None] * 4, [None] * 4
        for k in (3, 2):
            outs[k], pres[k] = ffn_backward(blocks[k], up_w, down_w, keep["u"][k])
        sent, came = scatter_far(*outs[2:])
        for k in (1, 0):
            outs[k], pres[k] = ffn_backward(blocks[k], up_w, down_w, keep["u"][k])
        parts = (outs[0], flip(outs[1], "c"), came)
        return parts, sent, pres

    def ffn_weight_grads(keep, blocks, pres, after):
        grad_down = transposed_dot(tie(keep["act"], after), blocks)
        grad_up = transposed_dot(tie(keep["ffn"], after), pres)
        return ffn_grad_rows(grad_up, grad_down)

    def ffn_grad_rows(grad_up, grad_down):
        rows = [
            grad_up[:, :half].reshape(rest, slab, half),
            grad_down[:half].reshape(rest, slab_half, model_width),
            grad_up[:, half:].reshape(rest, slab, half),
            grad_down[half:].reshape(rest, slab_half, model_width),
        ]
        return jnp.concatenate(rows, axis=1)

    def finish_ffn(depth, mine, other, stacks):
        if tiled:
            return ffn_grads(depth, place, mine, other, hidden_local, stacks)
        low, high = (jnp.where(c == k, mine, other) for k in (0, 1))
        up = jnp.concatenate([x[:, :slab].reshape(model_width, half) for x in (low, high)], axis=1)
        down = jnp.stack([x[:, slab:span].reshape(half, model_width) for x in (low, high)])
        new = (up.astype(F32), down.astype(F32))
        if stacks is None:
            return [jnp.stack([x] * LAYERS) for x in new]
        return [x.at[depth].set(y) for x, y in zip(stacks, new)]

    def attn_grad_rows(grad_mix, grad_out):
        rows = jnp.concatenate([grad_mix.astype(BF), grad_out.astype(BF)], axis=0)
        return rows.reshape(rest, slab_attn, model_width)

    def finish_attn(mine, other, first):
        end = first + slab_attn
        sums = jnp.where(at_home, mine[:, first:end], other[:, first:end])
        sums = sums.reshape(4 * local_width, model_width)
        mix = sums[: 3 * local_width].reshape(3, local_width, model_width)
        return mix.astype(F32), sums[3 * local_width :].astype(F32)

    def added(one, two):
        return (one.astype(F32) + two.astype(F32)).astype(BF)

    def attn_backward(keep, row_blocks):
        mix_w, out_w, _, _ = keep["weights"]
        return attend_backward(
            keep["mixed"], bias, mix_w, out_w, row_blocks, keep["attended"], keep["log_totals"]
        )

    def sum_first(x):
        return jnp.sum(x.astype(F32), axis=0)

    keep = saved[1]
    parts, sent, pres = ffn_blocks_backward(keep, down_blocks)
    ffn_a = exchange_rest(ffn_weight_grads(keep, down_blocks, pres, sent))
    grad, low, sums_11 = norm_backward(parts, keep["middle"], cotangent_home, ln_gain[1, 1])
    row_blocks = gather_start(low)

    own, core, plane, both = tie(last_parts, row_blocks)
    _, plane = scatter_far(plane, both)
    core = flip(core, "c")
    *parts, mix_grad, grad_out = tie(attn_backward(keep, row_blocks), plane, core, ffn_a)
    sent, came = scatter_far(*parts[2:])
    parts = (parts[0], flip(parts[1], "c"), came)
    grad_mix = dot(tie(mix_grad, sent).T, keep["x"])
    attn_a = attn_grad_rows(grad_mix, grad_out)
    grad, low, sums_10 = norm_backward(parts, keep["entry"], grad, ln_gain[1, 0])
    attn_a = exchange_rest(attn_a)

    down_blocks = gather_start(low)
    keep = saved[0]
    parts, sent, pres = ffn_blocks_backward(keep, down_blocks)
    ffn_b = ffn_weight_grads(keep, down_blocks, pres, sent)
    attn_a = sum_first(tie(attn_a, sent)).astype(BF)
    parts, ffn_b = tie((parts, ffn_b), attn_a)
    ffn_b = exchange_rest(ffn_b)
    grad, low, sums_01 = norm_backward(parts, keep["middle"], grad, ln_gain[0, 1])
    row_blocks = gather_start(low)
    plane, core = tie((plane, core), low)
    final = saved[1]["middle"] + own.astype(F32) + core.astype(F32) + plane.astype(F32)
    ffn_a = sum_first(tie(ffn_a, low)).astype(BF)
    held = jnp.concatenate([ffn_a[span:], attn_a], axis=0)
    came_a = flip(tie(held, low), "zh")

    *parts, mix_grad, grad_out = tie(attn_backward(keep, row_blocks), ffn_b, came_a)
    sent, came = scatter_far(*parts[2:])
    parts = (parts[0], flip(parts[1], "c"), came)
    ffn_b = sum_first(tie(ffn_b, sent))
    came_b = flip(ffn_b[span:].astype(BF), "zh")
    grad_mix = dot(tie(mix_grad, sent).T, keep["x"])
    attn_b = exchange_rest(attn_grad_rows(grad_mix, grad_out))
    parts = tie(parts, came_b)
    grad, low, sums_00 = norm_backward(parts, keep["entry"], grad, ln_gain[0, 0])

    first_of_four = (zh == 0) & (zl == 0)
    count = jnp.where(first_of_four, lengths[0], 0).astype(F32)
    sums = jnp.stack([sums_00, sums_01, sums_10, sums_11])
    small = jnp.concatenate(
        [
            sums[:, 0],
            sums[:, 1],
            jnp.broadcast_to(count, (1, model_width)),
            jnp.zeros((16 - 4 * LAYERS - 1, model_width), F32),
        ],
        axis=0,
    )
    small = small + flip(small, "zl")

    def in_two(x):
        high = lax.reduce_precision(x, 8, 7)
        return jnp.concatenate([high, x - high], axis=0).astype(BF)

    def from_two(x):
        high, rest_of_it = jnp.split(x.astype(F32), 2, axis=-2)
        return high + rest_of_it

    attn_b = sum_first(tie(attn_b, low)).astype(BF)
    sent_c = jnp.concatenate([attn_b, in_two(small)], axis=0)
    came_c = flip(sent_c, "zh")
    rows_b = spread_rest((ffn_b[:span] + came_b.astype(F32)).astype(BF), rest)
    small = small + from_two(came_c[slab_attn:])
    rows_a = jnp.concatenate(
        [
            added(jnp.concatenate([ffn_a[:span], attn_a], axis=0), tie(came_a, sent)),
            added(attn_b, came_c[:slab_attn]),
            in_two(small),
        ],
        axis=0,
    )
    rows_a = spread_rest(tie(rows_a, rows_b), rest)
    layer_out = rehome(tie(final.astype(BF), low))
    grad_tokens = rehome(low)
    row_ids = (2 * zh + zl) * rows_shard + jnp.arange(rows_shard, dtype=jnp.int32)
    live_rows = row_ids < lengths[0]
    logits = dot(layer_out, readout)
    top = jnp.max(logits, axis=-1, keepdims=True)
    log_total = top[:, 0] + jnp.log(jnp.sum(jnp.exp(logits - top), axis=-1))
    classes = jnp.arange(logits.shape[1], dtype=jnp.int32)
    picked = jnp.sum(jnp.where(labels[:, None] == classes[None, :], logits, 0.0), axis=-1)
    label_logprob = jnp.where(live_rows, picked - log_total, jnp.zeros_like(log_total))

    rows_b = (rows_b, flip(rows_b, "c"))
    ffn_stacks = finish_ffn(0, *rows_b, None)
    rows_a, ffn_stacks, layer_out, label_logprob, grad_tokens = tie(
        (rows_a, ffn_stacks, layer_out, label_logprob, grad_tokens)
    )
    rows_a = (rows_a, flip(rows_a, "c"))
    small = sum(jnp.sum(from_two(x[:, span + 2 * slab_attn :]), axis=0) for x in rows_a)
    grads_up, grads_down = finish_ffn(1, *rows_a, ffn_stacks)
    attn_a, attn_b = (finish_attn(*rows_a, span + k * slab_attn) for k in (0, 1))
    grads_mix, grads_out = (jnp.stack(pair) for pair in zip(attn_b, attn_a))
    grads_mix = jnp.transpose(grads_mix, (0, 3, 1, 2))
    grad_tokens = grad_tokens.astype(F32)
    gain_total = small[: 2 * LAYERS].reshape(LAYERS, 2, model_width)
    shift_total = small[2 * LAYERS : 4 * LAYERS].reshape(LAYERS, 2, model_width)
    token_count = small[4 * LAYERS, 0].astype(jnp.int32)
    return (
        layer_out,
        grad_tokens,
        gain_total,
        shift_total,
        grads_mix,
        grads_out,
        grads_up,
        grads_down.reshape(LAYERS, hidden_local, model_width),
        label_logprob,
        token_count,
    )


def solution(mesh):
    batch, model = mesh.devices.shape
    rest = batch // 2
    fine = Mesh(mesh.devices.reshape(rest, 2, 2, model // 2), ("r", "c", "zh", "zl"))
    dp = ("r", "c")
    mp = ("zh", "zl")
    both = dp + mp
    in_specs = (
        P(both, None),
        P(dp),
        P(dp, None),
        P(),
        P(),
        P(None, None, None, mp),
        P(None, mp, None),
        P(None, None, mp),
        P(None, mp, None),
        P(),
        P(both),
        P(both, None),
    )
    out_specs = (
        P(both, None),
        P(both, None),
        P(),
        P(),
        P(None, None, None, mp),
        P(None, mp, None),
        P(None, None, mp),
        P(None, mp, None),
        P(both),
        P(),
    )

    def body(*args):
        return local(*args, rest=rest)

    return jax.shard_map(body, mesh=fine, in_specs=in_specs, out_specs=out_specs, check_vma=False)
```

```python
import functools
import math

import jax
import jax.numpy as jnp
from jax import lax
from jax.experimental import pallas as pl
from jax.experimental.pallas import tpu as pltpu
from jax.sharding import Mesh, PartitionSpec as P

HD = 32
LAYERS = 2


EPS = 1e-05
NEG = -1000000000.0
ROOT_HALF = 0.7071067811865476
INV_ROOT_TAU = 0.3989422804014327
LOG2_E = 1.4426950408889634
VMEM_LIMIT = 56 * 1024 * 1024

BF = jnp.bfloat16
F32 = jnp.float32
FLIP = [(0, 1), (1, 0)]

HOME = []
for _c in range(2):
    for _h in range(2):
        for _p in range(2):
            _to = (_c, _h, _p) if _c == _h else (1 - _c, 1 - _h, _p)
            HOME.append((4 * _c + 2 * _h + _p, 4 * _to[0] + 2 * _to[1] + _to[2]))


def rehome(x):
    return lax.ppermute(x, ("c", "zh", "zl"), HOME)


def flip(x, axis):
    return lax.ppermute(x, axis, FLIP)


def tie(x, *before):
    return lax.optimization_barrier((x, before))[0]


def whole(*shape):
    return pl.BlockSpec(shape, lambda *_: (0,) * len(shape))


def kernel_params(micros):
    return dict(
        compiler_params=pltpu.CompilerParams(vmem_limit_bytes=VMEM_LIMIT),
        cost_estimate=pl.CostEstimate(
            flops=int(micros * 1.15e9), bytes_accessed=1 << 20, transcendentals=0
        ),
    )


def norm_unit(values):
    mean = jnp.mean(values, axis=-1, keepdims=True)
    centred = values - mean
    spread = jnp.mean(centred * centred, axis=-1, keepdims=True)
    inverse = lax.rsqrt(spread + EPS)
    return centred * inverse, inverse


def norm_forward_kernel(count, hidden_ref, *refs):
    parts = refs[:count]
    gain_ref, bias_ref, sum_ref, normed_ref = refs[count:]
    values = hidden_ref[...].astype(F32)
    for part in parts:
        values = values + part[...].astype(F32)
    sum_ref[...] = values
    unit, _ = norm_unit(values)
    normed_ref[...] = (unit * gain_ref[...] + bias_ref[...]).astype(BF)


def norm_forward(hidden, parts, gain, bias):
    rows, model = hidden.shape
    return pl.pallas_call(
        functools.partial(norm_forward_kernel, len(parts)),
        out_shape=[
            jax.ShapeDtypeStruct((rows, model), F32),
            jax.ShapeDtypeStruct((rows, model), BF),
        ],
        name="norm_forward",
        **kernel_params(6),
    )(hidden, *parts, gain[None], bias[None])


def norm_backward_kernel(
    own_ref, core_ref, plane_ref, values_ref, grad_ref, gain_ref, out_ref, low_ref, sums_ref
):
    grad_normed = own_ref[...].astype(F32) + core_ref[...].astype(F32) + plane_ref[...].astype(F32)
    unit, inverse = norm_unit(values_ref[...])
    scaled = grad_normed * gain_ref[...]
    mean_one = jnp.mean(scaled, axis=-1, keepdims=True)
    mean_two = jnp.mean(scaled * unit, axis=-1, keepdims=True)
    grad = grad_ref[...].astype(F32) + inverse * (scaled - mean_one - unit * mean_two)
    out_ref[...] = grad
    low_ref[...] = grad.astype(BF)
    sums_ref[0:1, :] = jnp.sum(grad_normed * unit, axis=0, keepdims=True)
    sums_ref[1:2, :] = jnp.sum(grad_normed, axis=0, keepdims=True)


def norm_backward(parts, values, grad, gain):
    rows, model = values.shape
    return pl.pallas_call(
        norm_backward_kernel,
        out_shape=[
            jax.ShapeDtypeStruct((rows, model), F32),
            jax.ShapeDtypeStruct((rows, model), BF),
            jax.ShapeDtypeStruct((2, model), F32),
        ],
        name="norm_backward",
        **kernel_params(3),
    )(*parts, values, grad, gain[None])


def gelu_and_slope(u):
    cdf = 0.5 * (1.0 + lax.erf(u * ROOT_HALF))
    return (u * cdf).astype(BF), cdf + u * jnp.exp(-0.5 * u * u) * INV_ROOT_TAU


def ffn_forward(x, up_w, down_w):
    u = dot(x, up_w)
    act = gelu_and_slope(u)[0]
    return dot(act, down_w).astype(BF), act, u


def ffn_backward(x, up_w, down_w, u):
    grad = (dot_nt(x, down_w) * gelu_and_slope(u)[1]).astype(BF)
    return dot_nt(grad, up_w).astype(BF), grad


def dot(left, right):
    return jnp.dot(left, right, preferred_element_type=F32)


def gather_start(x):
    plane = flip(x, "zl")
    return x, flip(x, "c"), plane, flip(plane, "c")


def scatter_far(plane, both):
    both = flip(both, "c")
    sent = (plane.astype(F32) + both.astype(F32)).astype(BF)
    return sent, flip(sent, "zl")


def exchange_rest(x):
    return lax.all_to_all(x, "r", 0, 0)


def spread_rest(x, count):
    return exchange_rest(jnp.broadcast_to(x[None], (count,) + x.shape))


def permute_rest(x, count):
    if count != 4:
        return spread_rest(x, count)
    r = lax.axis_index("r")
    pieces = [x] + [lax.ppermute(x, "r", [(i, i ^ k) for i in range(count)]) for k in range(1, count)]
    pieces = jnp.stack(pieces)
    return jnp.stack([lax.dynamic_index_in_dim(pieces, r ^ k, keepdims=False) for k in range(count)])


def weights_kernel(place_ref, up_home_ref, down_home_ref, far_ref, up_ref, down_ref):
    slab, half = up_home_ref.shape[1:]
    up_ref[:, :half] = up_home_ref[0]
    up_ref[:, half:] = far_ref[0, :slab]
    down_ref[0] = down_home_ref[0, 0]
    down_ref[1] = far_ref[0, slab:]


def ffn_weights_here(depth, place, w_up, w_down, far):
    model, hidden_local = w_up.shape[1:]
    half = hidden_local // 2
    count, span = far.shape[:2]
    slab, rows = model // count, half // count
    up, down = pl.pallas_call(
        weights_kernel,
        grid_spec=pltpu.PrefetchScalarGridSpec(
            num_scalar_prefetch=1,
            grid=(count,),
            in_specs=[
                pl.BlockSpec((1, slab, half), lambda j, p: (depth, j, p[0])),
                pl.BlockSpec((1, 1, rows, model), lambda j, p: (depth, p[0], j, 0)),
                pl.BlockSpec((1, span, model), lambda j, p: (j, 0, 0)),
            ],
            out_specs=[
                pl.BlockSpec((slab, hidden_local), lambda j, p: (j, 0)),
                pl.BlockSpec((2, rows, model), lambda j, p: (0, j, 0)),
            ],
        ),
        out_shape=[
            jax.ShapeDtypeStruct((model, hidden_local), BF),
            jax.ShapeDtypeStruct((2, half, model), BF),
        ],
        name="ffn_weights_here",
        **kernel_params(4),
    )(place, w_up, w_down.reshape(LAYERS, 2, half, model), far)
    return up, down.reshape(hidden_local, model)


def ffn_grads_kernel(place_ref, mine_ref, other_ref, *refs):
    up_ref, down_ref = refs[-2:]
    slab, half = up_ref.shape[1], up_ref.shape[2] // 2
    for low in range(2):

        @pl.when(place_ref[0] == low)
        def _(pair=(mine_ref, other_ref) if low == 0 else (other_ref, mine_ref)):
            for n, piece in enumerate(pair):
                up_ref[0, :, n * half : (n + 1) * half] = piece[0, :slab].astype(F32)
                down_ref[0, n] = piece[0, slab:].astype(F32)


def ffn_grads(depth, place, mine, other, hidden_local, stacks=None):
    half = hidden_local // 2
    count, _, model = mine.shape
    slab, rows = model // count, half // count
    span = slab + rows
    shapes = [(LAYERS, model, hidden_local), (LAYERS, 2, half, model)]
    held = [] if stacks is None else list(stacks)
    return pl.pallas_call(
        ffn_grads_kernel,
        grid_spec=pltpu.PrefetchScalarGridSpec(
            num_scalar_prefetch=1,
            grid=(count,),
            in_specs=[pl.BlockSpec((1, span, model), lambda j, p: (j, 0, 0))] * 2
            + [pl.BlockSpec(memory_space=pl.ANY)] * len(held),
            out_specs=[
                pl.BlockSpec((1, slab, hidden_local), lambda j, p: (depth, j, 0)),
                pl.BlockSpec((1, 2, rows, model), lambda j, p: (depth, 0, j, 0)),
            ],
        ),
        out_shape=[jax.ShapeDtypeStruct(shape, F32) for shape in shapes],
        input_output_aliases={3 + n: n for n in range(len(held))},
        name="ffn_grads",
        **kernel_params(4),
    )(place, mine, other, *held)


def dot_nt(left, right, **options):
    return lax.dot_general(
        left, right, (((1,), (1,)), ((), ())), preferred_element_type=F32, **options
    )


def attend_forward_kernel(
    heads,
    own_x_ref,
    core_x_ref,
    plane_x_ref,
    both_x_ref,
    mix_w_ref,
    bias_ref,
    out_w_ref,
    own_ref,
    core_ref,
    plane_ref,
    both_ref,
    x_ref,
    mix_ref,
    o_ref,
    lse_ref,
    q_scr,
    k_scr,
    vt_scr,
    e_scr,
    ot_scr,
):
    blk = bias_ref.shape[1]
    width = heads * HD
    step = pl.program_id(0)

    @pl.when(step == 0)
    def _():
        for n, ref in enumerate((own_x_ref, core_x_ref, plane_x_ref, both_x_ref)):
            rows = slice(n * (blk // 2), (n + 1) * (blk // 2))
            mix = dot_nt(ref[...], mix_w_ref[...]).astype(BF)
            x_ref[rows, :] = ref[...]
            mix_ref[rows, :] = mix
            q_scr[rows, :] = mix[:, :width]
            k_scr[rows, :] = mix[:, width : 2 * width]
            vt_scr[:, rows] = mix[:, 2 * width :].T

    q = q_scr[pl.ds(pl.multiple_of(step * blk, blk), blk), :]
    head_of = lax.broadcasted_iota(jnp.int32, q.shape, 1) // HD
    totals = []
    for h in range(heads):
        q_head = jnp.where(head_of == h, q, jnp.zeros_like(q))
        scores = dot_nt(k_scr[...], q_head) * (LOG2_E / math.sqrt(HD)) + bias_ref[...]
        top = jnp.max(scores, axis=0, keepdims=True)
        expo = jnp.exp2(scores - top)
        total = jnp.sum(expo, axis=0, keepdims=True)
        totals.append(total)
        e_scr[:, h * blk : (h + 1) * blk] = expo.astype(BF)
        lse_ref[h : h + 1, :] = top + jnp.log2(total)
    wide = dot(vt_scr[...], e_scr[...])
    for h in range(heads):
        ot_scr[h * HD : (h + 1) * HD, :] = (
            wide[h * HD : (h + 1) * HD, h * blk : (h + 1) * blk] / totals[h]
        )
    o = ot_scr[...].T
    o_ref[...] = o
    part = dot(o.astype(BF), out_w_ref[...]).astype(BF)

    @pl.when(step == 0)
    def _():
        own_ref[...] = part[: blk // 2]
        core_ref[...] = part[blk // 2 :]

    @pl.when(step == 1)
    def _():
        plane_ref[...] = part[: blk // 2]
        both_ref[...] = part[blk // 2 :]


def attend_forward(blocks, mix_w, bias, out_w):
    part_rows, model = blocks[0].shape
    blk, rows = 2 * part_rows, 4 * part_rows
    width3 = mix_w.shape[0]
    width = out_w.shape[0]
    heads = width // HD
    return pl.pallas_call(
        functools.partial(attend_forward_kernel, heads),
        grid=(2,),
        in_specs=[whole(part_rows, model)] * 4
        + [
            whole(width3, model),
            pl.BlockSpec((rows, blk), lambda i: (0, i)),
            whole(width, model),
        ],
        out_specs=[whole(part_rows, model)] * 4
        + [
            whole(rows, model),
            whole(rows, width3),
            pl.BlockSpec((blk, width), lambda i: (i, 0)),
            pl.BlockSpec((8, blk), lambda i: (0, i)),
        ],
        out_shape=[jax.ShapeDtypeStruct((part_rows, model), BF)] * 4
        + [
            jax.ShapeDtypeStruct((rows, model), BF),
            jax.ShapeDtypeStruct((rows, width3), BF),
            jax.ShapeDtypeStruct((rows, width), F32),
            jax.ShapeDtypeStruct((8, rows), F32),
        ],
        scratch_shapes=[
            pltpu.VMEM((rows, width), BF),
            pltpu.VMEM((rows, width), BF),
            pltpu.VMEM((width, rows), BF),
            pltpu.VMEM((rows, heads * blk), BF),
            pltpu.VMEM((width, blk), F32),
        ],
        name="attend_forward",
        **kernel_params(4),
    )(*blocks, mix_w, bias, out_w)


def attend_backward_kernel(
    heads,
    mix_ref,
    bias_ref,
    mix_w_ref,
    out_w_ref,
    row_refs,
    o_ref,
    lse_ref,
    part_refs,
    grad_ref,
    grad_out_ref,
    q_scr,
    k_scr,
    kt_scr,
    v_scr,
    do_scr,
    p_scr,
    ds_scr,
    qh_scr,
    doh_scr,
    dqt_scr,
    dk_scr,
    dv_scr,
):
    blk = bias_ref.shape[1]
    width = heads * HD
    step = pl.program_id(0)
    scale = 1.0 / math.sqrt(HD)

    @pl.when(step == 0)
    def _():
        q_scr[...] = mix_ref[:, :width]
        k_scr[...] = mix_ref[:, width : 2 * width]
        v_scr[...] = mix_ref[:, 2 * width :]
        kt_scr[...] = k_scr[...].T
        dk_scr[...] = jnp.zeros_like(dk_scr)
        dv_scr[...] = jnp.zeros_like(dv_scr)
        grad_out = jnp.zeros(grad_out_ref.shape, F32)
        for n, ref in enumerate(row_refs):
            rows = slice(n * blk, (n + 1) * blk)
            do_scr[rows, :] = dot_nt(ref[...], out_w_ref[...]).astype(BF)
            grad_out = grad_out + dot(o_ref[rows, :].astype(BF).T, ref[...])
        grad_out_ref[...] = grad_out

    rows = pl.ds(pl.multiple_of(step * blk, blk), blk)
    q = q_scr[rows, :]
    do = do_scr[rows, :]
    head_of = lax.broadcasted_iota(jnp.int32, q.shape, 1) // HD
    pick = (
        lax.broadcasted_iota(jnp.int32, (8, width), 1) // HD
        == lax.broadcasted_iota(jnp.int32, (8, width), 0)
    ).astype(F32)
    inner = dot_nt(pick, do.astype(F32) * o_ref[rows, :], precision=lax.Precision.HIGHEST)
    for h in range(heads):
        cols = slice(h * blk, (h + 1) * blk)
        q_head = jnp.where(head_of == h, q, jnp.zeros_like(q))
        do_head = jnp.where(head_of == h, do, jnp.zeros_like(do))
        qh_scr[cols, :] = q_head
        doh_scr[cols, :] = do_head
        scores = dot_nt(k_scr[...], q_head) * (LOG2_E * scale) + bias_ref[...]
        probs = jnp.exp2(scores - lse_ref[h : h + 1, :])
        p_scr[:, cols] = probs.astype(BF)
        ds = (probs * (dot_nt(v_scr[...], do_head) - inner[h : h + 1, :])).astype(BF)
        ds_scr[:, cols] = ds
    wide = dot(kt_scr[...], ds_scr[...])
    for h in range(heads):
        dqt_scr[h * HD : (h + 1) * HD, :] = (
            wide[h * HD : (h + 1) * HD, h * blk : (h + 1) * blk] * scale
        )
    dv_scr[...] += dot(p_scr[...], doh_scr[...])
    dk_scr[...] += dot(ds_scr[...], qh_scr[...])
    grad_ref[rows, :width] = dqt_scr[...].T.astype(BF)

    @pl.when(step == pl.num_programs(0) - 1)
    def _():
        grad_ref[:, width : 2 * width] = (dk_scr[...] * scale).astype(BF)
        grad_ref[:, 2 * width :] = dv_scr[...].astype(BF)
        for n, ref in enumerate(part_refs):
            ref[...] = dot(grad_ref[n * blk : (n + 1) * blk, :], mix_w_ref[...]).astype(BF)


def attend_backward(mix, bias, mix_w, out_w, rows_four, o, lse):
    rows, width3 = mix.shape
    blk = rows // 4
    width, model = out_w.shape
    heads = width // HD

    def kernel(*refs):
        attend_backward_kernel(
            heads, *refs[:4], refs[4:8], *refs[8:10], refs[10:14], *refs[14:]
        )

    return pl.pallas_call(
        kernel,
        grid=(4,),
        in_specs=[
            whole(rows, width3),
            pl.BlockSpec((rows, blk), lambda i: (0, i)),
            whole(width3, model),
            whole(width, model),
        ]
        + [whole(blk, model)] * 4
        + [whole(rows, width), pl.BlockSpec((8, blk), lambda i: (0, i))],
        out_specs=[whole(blk, model)] * 4 + [whole(rows, width3), whole(width, model)],
        out_shape=[jax.ShapeDtypeStruct((blk, model), BF)] * 4
        + [
            jax.ShapeDtypeStruct((rows, width3), BF),
            jax.ShapeDtypeStruct((width, model), F32),
        ],
        scratch_shapes=[
            pltpu.VMEM((rows, width), BF),
            pltpu.VMEM((rows, width), BF),
            pltpu.VMEM((width, rows), BF),
            pltpu.VMEM((rows, width), BF),
            pltpu.VMEM((rows, width), BF),
            pltpu.VMEM((rows, heads * blk), BF),
            pltpu.VMEM((rows, heads * blk), BF),
            pltpu.VMEM((heads * blk, width), BF),
            pltpu.VMEM((heads * blk, width), BF),
            pltpu.VMEM((width, blk), F32),
            pltpu.VMEM((rows, width), F32),
            pltpu.VMEM((rows, width), F32),
        ],
        name="attend_backward",
        **kernel_params(6),
    )(mix, bias, mix_w, out_w, *rows_four, o, lse)


def local(
    tokens,
    lengths,
    key_keep,
    ln_gain,
    ln_bias,
    w_qkv,
    w_out,
    w_up,
    w_down,
    readout,
    labels,
    cotangent,
    *,
    rest,
):
    rows_shard, model_width = tokens.shape
    seq_len = key_keep.shape[1]
    local_width = w_qkv.shape[3]
    hidden_local = w_up.shape[2]
    half = hidden_local // 2
    r = lax.axis_index("r")
    c = lax.axis_index("c")
    zh = lax.axis_index("zh")
    zl = lax.axis_index("zl")
    at_home = c == zh
    slab = model_width // rest
    slab_half = half // rest
    slab_attn = 4 * local_width // rest
    span = slab + slab_half

    hidden = rehome(tokens)
    mix_weights = jnp.transpose(w_qkv, (0, 2, 3, 1)).reshape(LAYERS, 3 * local_width, model_width)
    mix_first = rehome(mix_weights[0])
    out_first = rehome(w_out[0])
    place = c.astype(jnp.int32)[None]
    tiled = slab % 16 == 0 and slab_half % 16 == 0

    def far_ffn(depth):
        parts = [
            lax.dynamic_slice(w_up[depth], (r * slab, c * half), (slab, half)),
            lax.dynamic_slice(w_down[depth], (c * half + r * slab_half, 0), (slab_half, model_width)),
        ]
        return jnp.concatenate(parts, axis=0)

    def far_attn(depth):
        both = jnp.concatenate([mix_weights[depth], w_out[depth]], axis=0)
        return lax.dynamic_slice(both, (r * slab_attn, 0), (slab_attn, model_width))

    def ffn_weights(depth, far):
        if tiled:
            return ffn_weights_here(depth, place, w_up, w_down, far)
        up_home = lax.dynamic_slice(w_up[depth], (0, c * half), (model_width, half))
        up_far = far[:, :slab].reshape(model_width, half)
        down_home = lax.dynamic_slice(w_down[depth], (c * half, 0), (half, model_width))
        down_far = far[:, slab:].reshape(half, model_width)
        return (
            jnp.concatenate([up_home, up_far], axis=1),
            jnp.concatenate([down_home, down_far], axis=0),
        )

    def attn_weights(depth, far):
        far = far.reshape(4 * local_width, model_width)
        return (
            jnp.where(at_home, mix_weights[depth], far[: 3 * local_width]),
            jnp.where(at_home, w_out[depth], far[3 * local_width :]),
        )

    col_ids = jnp.arange(seq_len, dtype=jnp.int32)
    allowed = ((col_ids[None, :] < lengths[:, None]) & (key_keep == 1)).astype(jnp.int32)
    allowed = jnp.where(at_home, allowed, flip(allowed, "c")).reshape(2, 2, rows_shard)
    allowed = jnp.where(c == 1, allowed[::-1], allowed)
    allowed = jnp.where(zl == 1, allowed[:, ::-1], allowed)
    allowed = jnp.swapaxes(allowed, 0, 1).reshape(seq_len) == 1
    bias = jnp.where(allowed[:, None] | (col_ids[:, None] == col_ids[None, :]), 0.0, NEG)

    hidden = tie(hidden, bias)
    parts = ()
    saved = []
    for depth in range(LAYERS):
        first, last = depth == 0, depth == LAYERS - 1
        hidden, normed = norm_forward(hidden, parts, ln_gain[depth, 0], ln_bias[depth, 0])
        attn_blocks = gather_start(normed)
        if first:
            mix_w, out_w = mix_first, out_first
        else:
            mix_w, out_w = attn_weights(1, tie(attn_1, normed))
        if first:
            far_0 = tie(far_ffn(0), normed)
            attn_blocks = tie(attn_blocks, far_0)
            shadow = far_0 = flip(far_0, "zh")
        else:
            shadow = far_1 = flip(tie(far_ffn(1), attn_blocks[2]), "zh")
        *attn_parts, x, mixed, attended, log_totals = tie(
            attend_forward(attn_blocks, mix_w, bias, out_w), shadow
        )
        sent, came = scatter_far(*attn_parts[2:])
        attn_parts = (attn_parts[0], flip(attn_parts[1], "c"), came)
        if first:
            far_0 = spread_rest(tie(far_0, sent), rest)
            attn_1 = flip(tie(far_attn(1), sent), "zh")
            cotangent_home = rehome(tie(cotangent, normed))
        else:
            far_1 = spread_rest(tie(far_1, sent), rest)
        middle, normed_two = norm_forward(
            hidden, attn_parts, ln_gain[depth, 1], ln_bias[depth, 1]
        )
        ffn_blocks = gather_start(normed_two)
        if first:
            up_w, down_w = ffn_weights(depth, tie(far_0, normed_two))
        else:
            up_w, down_w = ffn_weights(depth, tie(far_1, normed_two))
        ffn_blocks = tie(ffn_blocks, up_w, down_w)
        if last:
            down_blocks = gather_start(tie(cotangent_home, ffn_blocks[2]))
        ffn_outs, acts, us = zip(*(ffn_forward(b, up_w, down_w) for b in ffn_blocks))
        own, core, plane, both = ffn_outs
        if first:
            plane, both = tie((plane, both), attn_1, cotangent_home)
            sent, came = scatter_far(plane, both)
            attn_1 = spread_rest(tie(attn_1, sent), rest)
            parts = (own, flip(core, "c"), came)
        saved.append(
            dict(
                entry=hidden,
                middle=middle,
                x=x,
                mixed=mixed,
                attended=attended,
                log_totals=log_totals,
                ffn=ffn_blocks,
                act=acts,
                u=us,
                weights=(mix_w, out_w, up_w, down_w),
            )
        )
        hidden = middle
    last_parts = (own, core, plane, both)

    def transposed_dot(left, right):
        left, right = (jnp.concatenate(x, axis=0) for x in (left, right))
        return dot(left.T, right).astype(BF)

    def ffn_blocks_backward(keep, blocks):
        _, _, up_w, down_w = keep["weights"]
        outs, pres = [None] * 4, [None] * 4
        for k in (3, 2):
            outs[k], pres[k] = ffn_backward(blocks[k], up_w, down_w, keep["u"][k])
        sent, came = scatter_far(*outs[2:])
        for k in (1, 0):
            outs[k], pres[k] = ffn_backward(blocks[k], up_w, down_w, keep["u"][k])
        parts = (outs[0], flip(outs[1], "c"), came)
        return parts, sent, pres

    def ffn_weight_grads(keep, blocks, pres, after):
        grad_down = transposed_dot(tie(keep["act"], after), blocks)
        grad_up = transposed_dot(tie(keep["ffn"], after), pres)
        return ffn_grad_rows(grad_up, grad_down)

    def ffn_grad_rows(grad_up, grad_down):
        rows = [
            grad_up[:, :half].reshape(rest, slab, half),
            grad_down[:half].reshape(rest, slab_half, model_width),
            grad_up[:, half:].reshape(rest, slab, half),
            grad_down[half:].reshape(rest, slab_half, model_width),
        ]
        return jnp.concatenate(rows, axis=1)

    def finish_ffn(depth, mine, other, stacks):
        if tiled:
            return ffn_grads(depth, place, mine, other, hidden_local, stacks)
        low, high = (jnp.where(c == k, mine, other) for k in (0, 1))
        up = jnp.concatenate([x[:, :slab].reshape(model_width, half) for x in (low, high)], axis=1)
        down = jnp.stack([x[:, slab:span].reshape(half, model_width) for x in (low, high)])
        new = (up.astype(F32), down.astype(F32))
        if stacks is None:
            return [jnp.stack([x] * LAYERS) for x in new]
        return [x.at[depth].set(y) for x, y in zip(stacks, new)]

    def attn_grad_rows(grad_mix, grad_out):
        rows = jnp.concatenate([grad_mix.astype(BF), grad_out.astype(BF)], axis=0)
        return rows.reshape(rest, slab_attn, model_width)

    def finish_attn(mine, other, first):
        end = first + slab_attn
        sums = jnp.where(at_home, mine[:, first:end], other[:, first:end])
        sums = sums.reshape(4 * local_width, model_width)
        mix = sums[: 3 * local_width].reshape(3, local_width, model_width)
        return mix.astype(F32), sums[3 * local_width :].astype(F32)

    def added(one, two):
        return (one.astype(F32) + two.astype(F32)).astype(BF)

    def attn_backward(keep, row_blocks):
        mix_w, out_w, _, _ = keep["weights"]
        return attend_backward(
            keep["mixed"], bias, mix_w, out_w, row_blocks, keep["attended"], keep["log_totals"]
        )

    def sum_first(x):
        return jnp.sum(x.astype(F32), axis=0)

    keep = saved[1]
    parts, sent, pres = ffn_blocks_backward(keep, down_blocks)
    ffn_a = exchange_rest(ffn_weight_grads(keep, down_blocks, pres, sent))
    grad, low, sums_11 = norm_backward(parts, keep["middle"], cotangent_home, ln_gain[1, 1])
    row_blocks = gather_start(low)

    own, core, plane, both = tie(last_parts, row_blocks)
    _, plane = scatter_far(plane, both)
    core = flip(core, "c")
    *parts, mix_grad, grad_out = tie(attn_backward(keep, row_blocks), plane, core, ffn_a)
    sent, came = scatter_far(*parts[2:])
    parts = (parts[0], flip(parts[1], "c"), came)
    grad_mix = dot(tie(mix_grad, sent).T, keep["x"])
    attn_a = attn_grad_rows(grad_mix, grad_out)
    grad, low, sums_10 = norm_backward(parts, keep["entry"], grad, ln_gain[1, 0])
    attn_a = exchange_rest(attn_a)

    down_blocks = gather_start(low)
    keep = saved[0]
    parts, sent, pres = ffn_blocks_backward(keep, down_blocks)
    ffn_b = ffn_weight_grads(keep, down_blocks, pres, sent)
    attn_a = sum_first(tie(attn_a, sent)).astype(BF)
    parts, ffn_b = tie((parts, ffn_b), attn_a)
    ffn_b = exchange_rest(ffn_b)
    grad, low, sums_01 = norm_backward(parts, keep["middle"], grad, ln_gain[0, 1])
    row_blocks = gather_start(low)
    plane, core = tie((plane, core), low)
    final = saved[1]["middle"] + own.astype(F32) + core.astype(F32) + plane.astype(F32)
    ffn_a = sum_first(tie(ffn_a, low)).astype(BF)
    held = jnp.concatenate([ffn_a[span:], attn_a], axis=0)
    came_a = flip(tie(held, low), "zh")

    *parts, mix_grad, grad_out = tie(attn_backward(keep, row_blocks), ffn_b, came_a)
    sent, came = scatter_far(*parts[2:])
    parts = (parts[0], flip(parts[1], "c"), came)
    ffn_b = sum_first(tie(ffn_b, sent))
    came_b = flip(ffn_b[span:].astype(BF), "zh")
    grad_mix = dot(tie(mix_grad, sent).T, keep["x"])
    attn_b = exchange_rest(attn_grad_rows(grad_mix, grad_out))
    parts = tie(parts, came_b)
    grad, low, sums_00 = norm_backward(parts, keep["entry"], grad, ln_gain[0, 0])

    first_of_four = (zh == 0) & (zl == 0)
    count = jnp.where(first_of_four, lengths[0], 0).astype(F32)
    sums = jnp.stack([sums_00, sums_01, sums_10, sums_11])
    small = jnp.concatenate(
        [
            sums[:, 0],
            sums[:, 1],
            jnp.broadcast_to(count, (1, model_width)),
            jnp.zeros((16 - 4 * LAYERS - 1, model_width), F32),
        ],
        axis=0,
    )
    small = small + flip(small, "zl")

    def in_two(x):
        high = lax.reduce_precision(x, 8, 7)
        return jnp.concatenate([high, x - high], axis=0).astype(BF)

    def from_two(x):
        high, rest_of_it = jnp.split(x.astype(F32), 2, axis=-2)
        return high + rest_of_it

    attn_b = sum_first(tie(attn_b, low)).astype(BF)
    sent_c = jnp.concatenate([attn_b, in_two(small)], axis=0)
    came_c = flip(sent_c, "zh")
    rows_b = spread_rest((ffn_b[:span] + came_b.astype(F32)).astype(BF), rest)
    small = small + from_two(came_c[slab_attn:])
    rows_a = jnp.concatenate(
        [
            added(jnp.concatenate([ffn_a[:span], attn_a], axis=0), tie(came_a, sent)),
            added(attn_b, came_c[:slab_attn]),
            in_two(small),
        ],
        axis=0,
    )
    rows_a = spread_rest(tie(rows_a, rows_b), rest)
    layer_out = rehome(tie(final.astype(BF), low))
    grad_tokens = rehome(low)
    row_ids = (2 * zh + zl) * rows_shard + jnp.arange(rows_shard, dtype=jnp.int32)
    live_rows = row_ids < lengths[0]
    logits = dot(layer_out, readout)
    top = jnp.max(logits, axis=-1, keepdims=True)
    log_total = top[:, 0] + jnp.log(jnp.sum(jnp.exp(logits - top), axis=-1))
    classes = jnp.arange(logits.shape[1], dtype=jnp.int32)
    picked = jnp.sum(jnp.where(labels[:, None] == classes[None, :], logits, 0.0), axis=-1)
    label_logprob = jnp.where(live_rows, picked - log_total, jnp.zeros_like(log_total))

    rows_b = (rows_b, flip(rows_b, "c"))
    ffn_stacks = finish_ffn(0, *rows_b, None)
    rows_a, ffn_stacks, layer_out, label_logprob, grad_tokens = tie(
        (rows_a, ffn_stacks, layer_out, label_logprob, grad_tokens)
    )
    rows_a = (rows_a, flip(rows_a, "c"))
    small = sum(jnp.sum(from_two(x[:, span + 2 * slab_attn :]), axis=0) for x in rows_a)
    grads_up, grads_down = finish_ffn(1, *rows_a, ffn_stacks)
    attn_a, attn_b = (finish_attn(*rows_a, span + k * slab_attn) for k in (0, 1))
    grads_mix, grads_out = (jnp.stack(pair) for pair in zip(attn_b, attn_a))
    grads_mix = jnp.transpose(grads_mix, (0, 3, 1, 2))
    grad_tokens = grad_tokens.astype(F32)
    gain_total = small[: 2 * LAYERS].reshape(LAYERS, 2, model_width)
    shift_total = small[2 * LAYERS : 4 * LAYERS].reshape(LAYERS, 2, model_width)
    token_count = small[4 * LAYERS, 0].astype(jnp.int32)
    return (
        layer_out,
        grad_tokens,
        gain_total,
        shift_total,
        grads_mix,
        grads_out,
        grads_up,
        grads_down.reshape(LAYERS, hidden_local, model_width),
        label_logprob,
        token_count,
    )


def solution(mesh):
    batch, model = mesh.devices.shape
    rest = batch // 2
    fine = Mesh(mesh.devices.reshape(rest, 2, 2, model // 2), ("r", "c", "zh", "zl"))
    dp = ("r", "c")
    mp = ("zh", "zl")
    both = dp + mp
    in_specs = (
        P(both, None),
        P(dp),
        P(dp, None),
        P(),
        P(),
        P(None, None, None, mp),
        P(None, mp, None),
        P(None, None, mp),
        P(None, mp, None),
        P(),
        P(both),
        P(both, None),
    )
    out_specs = (
        P(both, None),
        P(both, None),
        P(),
        P(),
        P(None, None, None, mp),
        P(None, mp, None),
        P(None, None, mp),
        P(None, mp, None),
        P(both),
        P(),
    )

    def body(*args):
        return local(*args, rest=rest)

    return jax.shard_map(body, mesh=fine, in_specs=in_specs, out_specs=out_specs, check_vma=False)
```

```python
import functools
import math

import jax
import jax.numpy as jnp
from jax import lax
from jax.experimental import pallas as pl
from jax.experimental.pallas import tpu as pltpu
from jax.sharding import Mesh, PartitionSpec as P

HD = 32
LAYERS = 2


EPS = 1e-05
NEG = -1000000000.0
ROOT_HALF = 0.7071067811865476
INV_ROOT_TAU = 0.3989422804014327
LOG2_E = 1.4426950408889634
VMEM_LIMIT = 56 * 1024 * 1024

BF = jnp.bfloat16
F32 = jnp.float32
FLIP = [(0, 1), (1, 0)]

HOME = []
for _c in range(2):
    for _h in range(2):
        for _p in range(2):
            _to = (_c, _h, _p) if _c == _h else (1 - _c, 1 - _h, _p)
            HOME.append((4 * _c + 2 * _h + _p, 4 * _to[0] + 2 * _to[1] + _to[2]))


def rehome(x):
    return lax.ppermute(x, ("c", "zh", "zl"), HOME)


def flip(x, axis):
    return lax.ppermute(x, axis, FLIP)


def tie(x, *before):
    return lax.optimization_barrier((x, before))[0]


def whole(*shape):
    return pl.BlockSpec(shape, lambda *_: (0,) * len(shape))


def kernel_params(micros):
    return dict(
        compiler_params=pltpu.CompilerParams(vmem_limit_bytes=VMEM_LIMIT),
        cost_estimate=pl.CostEstimate(
            flops=int(micros * 1.15e9), bytes_accessed=1 << 20, transcendentals=0
        ),
    )


def norm_unit(values):
    mean = jnp.mean(values, axis=-1, keepdims=True)
    centred = values - mean
    spread = jnp.mean(centred * centred, axis=-1, keepdims=True)
    inverse = lax.rsqrt(spread + EPS)
    return centred * inverse, inverse


def norm_forward_kernel(count, hidden_ref, *refs):
    parts = refs[:count]
    gain_ref, bias_ref, sum_ref, normed_ref = refs[count:]
    values = hidden_ref[...].astype(F32)
    for part in parts:
        values = values + part[...].astype(F32)
    sum_ref[...] = values
    unit, _ = norm_unit(values)
    normed_ref[...] = (unit * gain_ref[...] + bias_ref[...]).astype(BF)


def norm_forward(hidden, parts, gain, bias):
    rows, model = hidden.shape
    return pl.pallas_call(
        functools.partial(norm_forward_kernel, len(parts)),
        out_shape=[
            jax.ShapeDtypeStruct((rows, model), F32),
            jax.ShapeDtypeStruct((rows, model), BF),
        ],
        name="norm_forward",
        **kernel_params(6),
    )(hidden, *parts, gain[None], bias[None])


def norm_backward_kernel(
    own_ref, core_ref, plane_ref, values_ref, grad_ref, gain_ref, out_ref, low_ref, sums_ref
):
    grad_normed = own_ref[...].astype(F32) + core_ref[...].astype(F32) + plane_ref[...].astype(F32)
    unit, inverse = norm_unit(values_ref[...])
    scaled = grad_normed * gain_ref[...]
    mean_one = jnp.mean(scaled, axis=-1, keepdims=True)
    mean_two = jnp.mean(scaled * unit, axis=-1, keepdims=True)
    grad = grad_ref[...].astype(F32) + inverse * (scaled - mean_one - unit * mean_two)
    out_ref[...] = grad
    low_ref[...] = grad.astype(BF)
    sums_ref[0:1, :] = jnp.sum(grad_normed * unit, axis=0, keepdims=True)
    sums_ref[1:2, :] = jnp.sum(grad_normed, axis=0, keepdims=True)


def norm_backward(parts, values, grad, gain):
    rows, model = values.shape
    return pl.pallas_call(
        norm_backward_kernel,
        out_shape=[
            jax.ShapeDtypeStruct((rows, model), F32),
            jax.ShapeDtypeStruct((rows, model), BF),
            jax.ShapeDtypeStruct((2, model), F32),
        ],
        name="norm_backward",
        **kernel_params(3),
    )(*parts, values, grad, gain[None])


def gelu_and_slope(u):
    cdf = 0.5 * (1.0 + lax.erf(u * ROOT_HALF))
    return (u * cdf).astype(BF), cdf + u * jnp.exp(-0.5 * u * u) * INV_ROOT_TAU


def ffn_forward(x, up_w, down_w):
    u = dot(x, up_w)
    act = gelu_and_slope(u)[0]
    return dot(act, down_w).astype(BF), act, u


def ffn_backward(x, up_w, down_w, u):
    grad = (dot_nt(x, down_w) * gelu_and_slope(u)[1]).astype(BF)
    return dot_nt(grad, up_w).astype(BF), grad


def dot(left, right):
    return jnp.dot(left, right, preferred_element_type=F32)


def gather_start(x):
    plane = flip(x, "zl")
    return x, flip(x, "c"), plane, flip(plane, "c")


def scatter_far(plane, both):
    both = flip(both, "c")
    sent = (plane.astype(F32) + both.astype(F32)).astype(BF)
    return sent, flip(sent, "zl")


def exchange_rest(x):
    return lax.all_to_all(x, "r", 0, 0)


def spread_rest(x, count):
    return exchange_rest(jnp.broadcast_to(x[None], (count,) + x.shape))


def permute_rest(x, count):
    if count != 4:
        return spread_rest(x, count)
    r = lax.axis_index("r")
    pieces = [x] + [lax.ppermute(x, "r", [(i, i ^ k) for i in range(count)]) for k in range(1, count)]
    pieces = jnp.stack(pieces)
    return jnp.stack([lax.dynamic_index_in_dim(pieces, r ^ k, keepdims=False) for k in range(count)])


def weights_kernel(place_ref, up_home_ref, down_home_ref, far_ref, up_ref, down_ref):
    slab, half = up_home_ref.shape[1:]
    up_ref[:, :half] = up_home_ref[0]
    up_ref[:, half:] = far_ref[0, :slab]
    down_ref[0] = down_home_ref[0, 0]
    down_ref[1] = far_ref[0, slab:]


def ffn_weights_here(depth, place, w_up, w_down, far):
    model, hidden_local = w_up.shape[1:]
    half = hidden_local // 2
    count, span = far.shape[:2]
    slab, rows = model // count, half // count
    up, down = pl.pallas_call(
        weights_kernel,
        grid_spec=pltpu.PrefetchScalarGridSpec(
            num_scalar_prefetch=1,
            grid=(count,),
            in_specs=[
                pl.BlockSpec((1, slab, half), lambda j, p: (depth, j, p[0])),
                pl.BlockSpec((1, 1, rows, model), lambda j, p: (depth, p[0], j, 0)),
                pl.BlockSpec((1, span, model), lambda j, p: (j, 0, 0)),
            ],
            out_specs=[
                pl.BlockSpec((slab, hidden_local), lambda j, p: (j, 0)),
                pl.BlockSpec((2, rows, model), lambda j, p: (0, j, 0)),
            ],
        ),
        out_shape=[
            jax.ShapeDtypeStruct((model, hidden_local), BF),
            jax.ShapeDtypeStruct((2, half, model), BF),
        ],
        name="ffn_weights_here",
        **kernel_params(4),
    )(place, w_up, w_down.reshape(LAYERS, 2, half, model), far)
    return up, down.reshape(hidden_local, model)


def ffn_grads_kernel(place_ref, mine_ref, other_ref, *refs):
    up_ref, down_ref = refs[-2:]
    slab, half = up_ref.shape[1], up_ref.shape[2] // 2
    for low in range(2):

        @pl.when(place_ref[0] == low)
        def _(pair=(mine_ref, other_ref) if low == 0 else (other_ref, mine_ref)):
            for n, piece in enumerate(pair):
                up_ref[0, :, n * half : (n + 1) * half] = piece[0, :slab].astype(F32)
                down_ref[0, n] = piece[0, slab:].astype(F32)


def ffn_grads(depth, place, mine, other, hidden_local, stacks=None):
    half = hidden_local // 2
    count, _, model = mine.shape
    slab, rows = model // count, half // count
    span = slab + rows
    shapes = [(LAYERS, model, hidden_local), (LAYERS, 2, half, model)]
    held = [] if stacks is None else list(stacks)
    return pl.pallas_call(
        ffn_grads_kernel,
        grid_spec=pltpu.PrefetchScalarGridSpec(
            num_scalar_prefetch=1,
            grid=(count,),
            in_specs=[pl.BlockSpec((1, span, model), lambda j, p: (j, 0, 0))] * 2
            + [pl.BlockSpec(memory_space=pl.ANY)] * len(held),
            out_specs=[
                pl.BlockSpec((1, slab, hidden_local), lambda j, p: (depth, j, 0)),
                pl.BlockSpec((1, 2, rows, model), lambda j, p: (depth, 0, j, 0)),
            ],
        ),
        out_shape=[jax.ShapeDtypeStruct(shape, F32) for shape in shapes],
        input_output_aliases={3 + n: n for n in range(len(held))},
        name="ffn_grads",
        **kernel_params(4),
    )(place, mine, other, *held)


def dot_nt(left, right, **options):
    return lax.dot_general(
        left, right, (((1,), (1,)), ((), ())), preferred_element_type=F32, **options
    )


def attend_forward_kernel(
    heads,
    own_x_ref,
    core_x_ref,
    plane_x_ref,
    both_x_ref,
    mix_w_ref,
    bias_ref,
    out_w_ref,
    own_ref,
    core_ref,
    plane_ref,
    both_ref,
    x_ref,
    mix_ref,
    o_ref,
    lse_ref,
    q_scr,
    k_scr,
    vt_scr,
    e_scr,
    ot_scr,
):
    blk = bias_ref.shape[1]
    width = heads * HD
    step = pl.program_id(0)

    @pl.when(step == 0)
    def _():
        for n, ref in enumerate((own_x_ref, core_x_ref, plane_x_ref, both_x_ref)):
            rows = slice(n * (blk // 2), (n + 1) * (blk // 2))
            mix = dot_nt(ref[...], mix_w_ref[...]).astype(BF)
            x_ref[rows, :] = ref[...]
            mix_ref[rows, :] = mix
            q_scr[rows, :] = mix[:, :width]
            k_scr[rows, :] = mix[:, width : 2 * width]
            vt_scr[:, rows] = mix[:, 2 * width :].T

    q = q_scr[pl.ds(pl.multiple_of(step * blk, blk), blk), :]
    head_of = lax.broadcasted_iota(jnp.int32, q.shape, 1) // HD
    totals = []
    for h in range(heads):
        q_head = jnp.where(head_of == h, q, jnp.zeros_like(q))
        scores = dot_nt(k_scr[...], q_head) * (LOG2_E / math.sqrt(HD)) + bias_ref[...]
        top = jnp.max(scores, axis=0, keepdims=True)
        expo = jnp.exp2(scores - top)
        total = jnp.sum(expo, axis=0, keepdims=True)
        totals.append(total)
        e_scr[:, h * blk : (h + 1) * blk] = expo.astype(BF)
        lse_ref[h : h + 1, :] = top + jnp.log2(total)
    wide = dot(vt_scr[...], e_scr[...])
    for h in range(heads):
        ot_scr[h * HD : (h + 1) * HD, :] = (
            wide[h * HD : (h + 1) * HD, h * blk : (h + 1) * blk] / totals[h]
        )
    o = ot_scr[...].T
    o_ref[...] = o
    part = dot(o.astype(BF), out_w_ref[...]).astype(BF)

    @pl.when(step == 0)
    def _():
        own_ref[...] = part[: blk // 2]
        core_ref[...] = part[blk // 2 :]

    @pl.when(step == 1)
    def _():
        plane_ref[...] = part[: blk // 2]
        both_ref[...] = part[blk // 2 :]


def attend_forward(blocks, mix_w, bias, out_w):
    part_rows, model = blocks[0].shape
    blk, rows = 2 * part_rows, 4 * part_rows
    width3 = mix_w.shape[0]
    width = out_w.shape[0]
    heads = width // HD
    return pl.pallas_call(
        functools.partial(attend_forward_kernel, heads),
        grid=(2,),
        in_specs=[whole(part_rows, model)] * 4
        + [
            whole(width3, model),
            pl.BlockSpec((rows, blk), lambda i: (0, i)),
            whole(width, model),
        ],
        out_specs=[whole(part_rows, model)] * 4
        + [
            whole(rows, model),
            whole(rows, width3),
            pl.BlockSpec((blk, width), lambda i: (i, 0)),
            pl.BlockSpec((8, blk), lambda i: (0, i)),
        ],
        out_shape=[jax.ShapeDtypeStruct((part_rows, model), BF)] * 4
        + [
            jax.ShapeDtypeStruct((rows, model), BF),
            jax.ShapeDtypeStruct((rows, width3), BF),
            jax.ShapeDtypeStruct((rows, width), F32),
            jax.ShapeDtypeStruct((8, rows), F32),
        ],
        scratch_shapes=[
            pltpu.VMEM((rows, width), BF),
            pltpu.VMEM((rows, width), BF),
            pltpu.VMEM((width, rows), BF),
            pltpu.VMEM((rows, heads * blk), BF),
            pltpu.VMEM((width, blk), F32),
        ],
        name="attend_forward",
        **kernel_params(4),
    )(*blocks, mix_w, bias, out_w)


def attend_backward_kernel(
    heads,
    mix_ref,
    bias_ref,
    mix_w_ref,
    out_w_ref,
    row_refs,
    o_ref,
    lse_ref,
    part_refs,
    grad_ref,
    grad_out_ref,
    q_scr,
    k_scr,
    kt_scr,
    v_scr,
    do_scr,
    p_scr,
    ds_scr,
    qh_scr,
    doh_scr,
    dqt_scr,
    dk_scr,
    dv_scr,
):
    blk = bias_ref.shape[1]
    width = heads * HD
    step = pl.program_id(0)
    scale = 1.0 / math.sqrt(HD)

    @pl.when(step == 0)
    def _():
        q_scr[...] = mix_ref[:, :width]
        k_scr[...] = mix_ref[:, width : 2 * width]
        v_scr[...] = mix_ref[:, 2 * width :]
        kt_scr[...] = k_scr[...].T
        dk_scr[...] = jnp.zeros_like(dk_scr)
        dv_scr[...] = jnp.zeros_like(dv_scr)
        grad_out = jnp.zeros(grad_out_ref.shape, F32)
        for n, ref in enumerate(row_refs):
            rows = slice(n * blk, (n + 1) * blk)
            do_scr[rows, :] = dot_nt(ref[...], out_w_ref[...]).astype(BF)
            grad_out = grad_out + dot(o_ref[rows, :].astype(BF).T, ref[...])
        grad_out_ref[...] = grad_out

    rows = pl.ds(pl.multiple_of(step * blk, blk), blk)
    q = q_scr[rows, :]
    do = do_scr[rows, :]
    head_of = lax.broadcasted_iota(jnp.int32, q.shape, 1) // HD
    pick = (
        lax.broadcasted_iota(jnp.int32, (8, width), 1) // HD
        == lax.broadcasted_iota(jnp.int32, (8, width), 0)
    ).astype(F32)
    inner = dot_nt(pick, do.astype(F32) * o_ref[rows, :], precision=lax.Precision.HIGHEST)
    for h in range(heads):
        cols = slice(h * blk, (h + 1) * blk)
        q_head = jnp.where(head_of == h, q, jnp.zeros_like(q))
        do_head = jnp.where(head_of == h, do, jnp.zeros_like(do))
        qh_scr[cols, :] = q_head
        doh_scr[cols, :] = do_head
        scores = dot_nt(k_scr[...], q_head) * (LOG2_E * scale) + bias_ref[...]
        probs = jnp.exp2(scores - lse_ref[h : h + 1, :])
        p_scr[:, cols] = probs.astype(BF)
        ds = (probs * (dot_nt(v_scr[...], do_head) - inner[h : h + 1, :])).astype(BF)
        ds_scr[:, cols] = ds
    wide = dot(kt_scr[...], ds_scr[...])
    for h in range(heads):
        dqt_scr[h * HD : (h + 1) * HD, :] = (
            wide[h * HD : (h + 1) * HD, h * blk : (h + 1) * blk] * scale
        )
    dv_scr[...] += dot(p_scr[...], doh_scr[...])
    dk_scr[...] += dot(ds_scr[...], qh_scr[...])
    grad_ref[rows, :width] = dqt_scr[...].T.astype(BF)

    @pl.when(step == pl.num_programs(0) - 1)
    def _():
        grad_ref[:, width : 2 * width] = (dk_scr[...] * scale).astype(BF)
        grad_ref[:, 2 * width :] = dv_scr[...].astype(BF)
        for n, ref in enumerate(part_refs):
            ref[...] = dot(grad_ref[n * blk : (n + 1) * blk, :], mix_w_ref[...]).astype(BF)


def attend_backward(mix, bias, mix_w, out_w, rows_four, o, lse):
    rows, width3 = mix.shape
    blk = rows // 4
    width, model = out_w.shape
    heads = width // HD

    def kernel(*refs):
        attend_backward_kernel(
            heads, *refs[:4], refs[4:8], *refs[8:10], refs[10:14], *refs[14:]
        )

    return pl.pallas_call(
        kernel,
        grid=(4,),
        in_specs=[
            whole(rows, width3),
            pl.BlockSpec((rows, blk), lambda i: (0, i)),
            whole(width3, model),
            whole(width, model),
        ]
        + [whole(blk, model)] * 4
        + [whole(rows, width), pl.BlockSpec((8, blk), lambda i: (0, i))],
        out_specs=[whole(blk, model)] * 4 + [whole(rows, width3), whole(width, model)],
        out_shape=[jax.ShapeDtypeStruct((blk, model), BF)] * 4
        + [
            jax.ShapeDtypeStruct((rows, width3), BF),
            jax.ShapeDtypeStruct((width, model), F32),
        ],
        scratch_shapes=[
            pltpu.VMEM((rows, width), BF),
            pltpu.VMEM((rows, width), BF),
            pltpu.VMEM((width, rows), BF),
            pltpu.VMEM((rows, width), BF),
            pltpu.VMEM((rows, width), BF),
            pltpu.VMEM((rows, heads * blk), BF),
            pltpu.VMEM((rows, heads * blk), BF),
            pltpu.VMEM((heads * blk, width), BF),
            pltpu.VMEM((heads * blk, width), BF),
            pltpu.VMEM((width, blk), F32),
            pltpu.VMEM((rows, width), F32),
            pltpu.VMEM((rows, width), F32),
        ],
        name="attend_backward",
        **kernel_params(6),
    )(mix, bias, mix_w, out_w, *rows_four, o, lse)


def local(
    tokens,
    lengths,
    key_keep,
    ln_gain,
    ln_bias,
    w_qkv,
    w_out,
    w_up,
    w_down,
    readout,
    labels,
    cotangent,
    *,
    rest,
):
    rows_shard, model_width = tokens.shape
    seq_len = key_keep.shape[1]
    local_width = w_qkv.shape[3]
    hidden_local = w_up.shape[2]
    half = hidden_local // 2
    r = lax.axis_index("r")
    c = lax.axis_index("c")
    zh = lax.axis_index("zh")
    zl = lax.axis_index("zl")
    at_home = c == zh
    slab = model_width // rest
    slab_half = half // rest
    slab_attn = 4 * local_width // rest
    span = slab + slab_half

    hidden = rehome(tokens)
    mix_weights = jnp.transpose(w_qkv, (0, 2, 3, 1)).reshape(LAYERS, 3 * local_width, model_width)
    mix_first = rehome(mix_weights[0])
    out_first = rehome(w_out[0])
    place = c.astype(jnp.int32)[None]
    tiled = slab % 16 == 0 and slab_half % 16 == 0

    def far_ffn(depth):
        parts = [
            lax.dynamic_slice(w_up[depth], (r * slab, c * half), (slab, half)),
            lax.dynamic_slice(w_down[depth], (c * half + r * slab_half, 0), (slab_half, model_width)),
        ]
        return jnp.concatenate(parts, axis=0)

    def far_attn(depth):
        both = jnp.concatenate([mix_weights[depth], w_out[depth]], axis=0)
        return lax.dynamic_slice(both, (r * slab_attn, 0), (slab_attn, model_width))

    def ffn_weights(depth, far):
        if tiled:
            return ffn_weights_here(depth, place, w_up, w_down, far)
        up_home = lax.dynamic_slice(w_up[depth], (0, c * half), (model_width, half))
        up_far = far[:, :slab].reshape(model_width, half)
        down_home = lax.dynamic_slice(w_down[depth], (c * half, 0), (half, model_width))
        down_far = far[:, slab:].reshape(half, model_width)
        return (
            jnp.concatenate([up_home, up_far], axis=1),
            jnp.concatenate([down_home, down_far], axis=0),
        )

    def attn_weights(depth, far):
        far = far.reshape(4 * local_width, model_width)
        return (
            jnp.where(at_home, mix_weights[depth], far[: 3 * local_width]),
            jnp.where(at_home, w_out[depth], far[3 * local_width :]),
        )

    col_ids = jnp.arange(seq_len, dtype=jnp.int32)
    allowed = ((col_ids[None, :] < lengths[:, None]) & (key_keep == 1)).astype(jnp.int32)
    allowed = jnp.where(at_home, allowed, flip(allowed, "c")).reshape(2, 2, rows_shard)
    allowed = jnp.where(c == 1, allowed[::-1], allowed)
    allowed = jnp.where(zl == 1, allowed[:, ::-1], allowed)
    allowed = jnp.swapaxes(allowed, 0, 1).reshape(seq_len) == 1
    bias = jnp.where(allowed[:, None] | (col_ids[:, None] == col_ids[None, :]), 0.0, NEG)

    hidden = tie(hidden, bias)
    parts = ()
    saved = []
    for depth in range(LAYERS):
        first, last = depth == 0, depth == LAYERS - 1
        hidden, normed = norm_forward(hidden, parts, ln_gain[depth, 0], ln_bias[depth, 0])
        attn_blocks = gather_start(normed)
        if first:
            mix_w, out_w = mix_first, out_first
        else:
            mix_w, out_w = attn_weights(1, tie(attn_1, normed))
        if first:
            far_0 = tie(far_ffn(0), normed)
            attn_blocks = tie(attn_blocks, far_0)
            shadow = far_0 = flip(far_0, "zh")
        else:
            shadow = far_1 = flip(tie(far_ffn(1), attn_blocks[2]), "zh")
        *attn_parts, x, mixed, attended, log_totals = tie(
            attend_forward(attn_blocks, mix_w, bias, out_w), shadow
        )
        sent, came = scatter_far(*attn_parts[2:])
        attn_parts = (attn_parts[0], flip(attn_parts[1], "c"), came)
        if first:
            far_0 = spread_rest(tie(far_0, attn_parts[1]), rest)
            attn_1 = flip(tie(far_attn(1), sent), "zh")
            cotangent_home = rehome(tie(cotangent, normed))
        else:
            far_1 = spread_rest(tie(far_1, attn_parts[1]), rest)
        middle, normed_two = norm_forward(
            hidden, attn_parts, ln_gain[depth, 1], ln_bias[depth, 1]
        )
        ffn_blocks = gather_start(normed_two)
        if first:
            up_w, down_w = ffn_weights(depth, tie(far_0, normed_two))
        else:
            up_w, down_w = ffn_weights(depth, tie(far_1, normed_two))
        ffn_blocks = tie(ffn_blocks, up_w, down_w)
        if last:
            down_blocks = gather_start(tie(cotangent_home, ffn_blocks[2]))
        ffn_outs, acts, us = zip(*(ffn_forward(b, up_w, down_w) for b in ffn_blocks))
        own, core, plane, both = ffn_outs
        if first:
            plane, both = tie((plane, both), attn_1, cotangent_home)
            sent, came = scatter_far(plane, both)
            attn_1 = spread_rest(tie(attn_1, sent), rest)
            parts = (own, flip(core, "c"), came)
        saved.append(
            dict(
                entry=hidden,
                middle=middle,
                x=x,
                mixed=mixed,
                attended=attended,
                log_totals=log_totals,
                ffn=ffn_blocks,
                act=acts,
                u=us,
                weights=(mix_w, out_w, up_w, down_w),
            )
        )
        hidden = middle
    last_parts = (own, core, plane, both)

    def transposed_dot(left, right):
        left, right = (jnp.concatenate(x, axis=0) for x in (left, right))
        return dot(left.T, right).astype(BF)

    def ffn_blocks_backward(keep, blocks):
        _, _, up_w, down_w = keep["weights"]
        outs, pres = [None] * 4, [None] * 4
        for k in (3, 2):
            outs[k], pres[k] = ffn_backward(blocks[k], up_w, down_w, keep["u"][k])
        sent, came = scatter_far(*outs[2:])
        for k in (1, 0):
            outs[k], pres[k] = ffn_backward(blocks[k], up_w, down_w, keep["u"][k])
        parts = (outs[0], flip(outs[1], "c"), came)
        return parts, sent, pres

    def ffn_weight_grads(keep, blocks, pres, after):
        grad_down = transposed_dot(tie(keep["act"], after), blocks)
        grad_up = transposed_dot(tie(keep["ffn"], after), pres)
        return ffn_grad_rows(grad_up, grad_down)

    def ffn_grad_rows(grad_up, grad_down):
        rows = [
            grad_up[:, :half].reshape(rest, slab, half),
            grad_down[:half].reshape(rest, slab_half, model_width),
            grad_up[:, half:].reshape(rest, slab, half),
            grad_down[half:].reshape(rest, slab_half, model_width),
        ]
        return jnp.concatenate(rows, axis=1)

    def finish_ffn(depth, mine, other, stacks):
        if tiled:
            return ffn_grads(depth, place, mine, other, hidden_local, stacks)
        low, high = (jnp.where(c == k, mine, other) for k in (0, 1))
        up = jnp.concatenate([x[:, :slab].reshape(model_width, half) for x in (low, high)], axis=1)
        down = jnp.stack([x[:, slab:span].reshape(half, model_width) for x in (low, high)])
        new = (up.astype(F32), down.astype(F32))
        if stacks is None:
            return [jnp.stack([x] * LAYERS) for x in new]
        return [x.at[depth].set(y) for x, y in zip(stacks, new)]

    def attn_grad_rows(grad_mix, grad_out):
        rows = jnp.concatenate([grad_mix.astype(BF), grad_out.astype(BF)], axis=0)
        return rows.reshape(rest, slab_attn, model_width)

    def finish_attn(mine, other, first):
        end = first + slab_attn
        sums = jnp.where(at_home, mine[:, first:end], other[:, first:end])
        sums = sums.reshape(4 * local_width, model_width)
        mix = sums[: 3 * local_width].reshape(3, local_width, model_width)
        return mix.astype(F32), sums[3 * local_width :].astype(F32)

    def added(one, two):
        return (one.astype(F32) + two.astype(F32)).astype(BF)

    def attn_backward(keep, row_blocks):
        mix_w, out_w, _, _ = keep["weights"]
        return attend_backward(
            keep["mixed"], bias, mix_w, out_w, row_blocks, keep["attended"], keep["log_totals"]
        )

    def sum_first(x):
        return jnp.sum(x.astype(F32), axis=0)

    keep = saved[1]
    parts, sent, pres = ffn_blocks_backward(keep, down_blocks)
    ffn_a = exchange_rest(ffn_weight_grads(keep, down_blocks, pres, sent))
    grad, low, sums_11 = norm_backward(parts, keep["middle"], cotangent_home, ln_gain[1, 1])
    row_blocks = gather_start(low)

    own, core, plane, both = tie(last_parts, row_blocks)
    _, plane = scatter_far(plane, both)
    core = flip(core, "c")
    *parts, mix_grad, grad_out = tie(attn_backward(keep, row_blocks), plane, core, ffn_a)
    sent, came = scatter_far(*parts[2:])
    parts = (parts[0], flip(parts[1], "c"), came)
    grad_mix = dot(tie(mix_grad, sent).T, keep["x"])
    attn_a = attn_grad_rows(grad_mix, grad_out)
    grad, low, sums_10 = norm_backward(parts, keep["entry"], grad, ln_gain[1, 0])
    attn_a = exchange_rest(attn_a)

    down_blocks = gather_start(low)
    keep = saved[0]
    parts, sent, pres = ffn_blocks_backward(keep, down_blocks)
    ffn_b = ffn_weight_grads(keep, down_blocks, pres, sent)
    attn_a = sum_first(tie(attn_a, sent)).astype(BF)
    parts, ffn_b = tie((parts, ffn_b), attn_a)
    ffn_b = exchange_rest(ffn_b)
    grad, low, sums_01 = norm_backward(parts, keep["middle"], grad, ln_gain[0, 1])
    row_blocks = gather_start(low)
    plane, core = tie((plane, core), low)
    final = saved[1]["middle"] + own.astype(F32) + core.astype(F32) + plane.astype(F32)
    ffn_a = sum_first(tie(ffn_a, low)).astype(BF)
    held = jnp.concatenate([ffn_a[span:], attn_a], axis=0)
    came_a = flip(tie(held, low), "zh")

    *parts, mix_grad, grad_out = tie(attn_backward(keep, row_blocks), ffn_b, came_a)
    sent, came = scatter_far(*parts[2:])
    parts = (parts[0], flip(parts[1], "c"), came)
    ffn_b = sum_first(tie(ffn_b, sent))
    came_b = flip(ffn_b[span:].astype(BF), "zh")
    grad_mix = dot(tie(mix_grad, sent).T, keep["x"])
    attn_b = exchange_rest(attn_grad_rows(grad_mix, grad_out))
    parts = tie(parts, came_b)
    grad, low, sums_00 = norm_backward(parts, keep["entry"], grad, ln_gain[0, 0])

    first_of_four = (zh == 0) & (zl == 0)
    count = jnp.where(first_of_four, lengths[0], 0).astype(F32)
    sums = jnp.stack([sums_00, sums_01, sums_10, sums_11])
    small = jnp.concatenate(
        [
            sums[:, 0],
            sums[:, 1],
            jnp.broadcast_to(count, (1, model_width)),
            jnp.zeros((16 - 4 * LAYERS - 1, model_width), F32),
        ],
        axis=0,
    )
    small = small + flip(small, "zl")

    def in_two(x):
        high = lax.reduce_precision(x, 8, 7)
        return jnp.concatenate([high, x - high], axis=0).astype(BF)

    def from_two(x):
        high, rest_of_it = jnp.split(x.astype(F32), 2, axis=-2)
        return high + rest_of_it

    attn_b = sum_first(tie(attn_b, low)).astype(BF)
    sent_c = jnp.concatenate([attn_b, in_two(small)], axis=0)
    came_c = flip(sent_c, "zh")
    rows_b = spread_rest((ffn_b[:span] + came_b.astype(F32)).astype(BF), rest)
    small = small + from_two(came_c[slab_attn:])
    rows_a = jnp.concatenate(
        [
            added(jnp.concatenate([ffn_a[:span], attn_a], axis=0), tie(came_a, sent)),
            added(attn_b, came_c[:slab_attn]),
            in_two(small),
        ],
        axis=0,
    )
    rows_a = spread_rest(tie(rows_a, rows_b), rest)
    layer_out = rehome(tie(final.astype(BF), low))
    grad_tokens = rehome(low)
    row_ids = (2 * zh + zl) * rows_shard + jnp.arange(rows_shard, dtype=jnp.int32)
    live_rows = row_ids < lengths[0]
    logits = dot(layer_out, readout)
    top = jnp.max(logits, axis=-1, keepdims=True)
    log_total = top[:, 0] + jnp.log(jnp.sum(jnp.exp(logits - top), axis=-1))
    classes = jnp.arange(logits.shape[1], dtype=jnp.int32)
    picked = jnp.sum(jnp.where(labels[:, None] == classes[None, :], logits, 0.0), axis=-1)
    label_logprob = jnp.where(live_rows, picked - log_total, jnp.zeros_like(log_total))

    rows_b = (rows_b, flip(rows_b, "c"))
    ffn_stacks = finish_ffn(0, *rows_b, None)
    rows_a, ffn_stacks, layer_out, label_logprob, grad_tokens = tie(
        (rows_a, ffn_stacks, layer_out, label_logprob, grad_tokens)
    )
    rows_a = (rows_a, flip(rows_a, "c"))
    small = sum(jnp.sum(from_two(x[:, span + 2 * slab_attn :]), axis=0) for x in rows_a)
    grads_up, grads_down = finish_ffn(1, *rows_a, ffn_stacks)
    attn_a, attn_b = (finish_attn(*rows_a, span + k * slab_attn) for k in (0, 1))
    grads_mix, grads_out = (jnp.stack(pair) for pair in zip(attn_b, attn_a))
    grads_mix = jnp.transpose(grads_mix, (0, 3, 1, 2))
    grad_tokens = grad_tokens.astype(F32)
    gain_total = small[: 2 * LAYERS].reshape(LAYERS, 2, model_width)
    shift_total = small[2 * LAYERS : 4 * LAYERS].reshape(LAYERS, 2, model_width)
    token_count = small[4 * LAYERS, 0].astype(jnp.int32)
    return (
        layer_out,
        grad_tokens,
        gain_total,
        shift_total,
        grads_mix,
        grads_out,
        grads_up,
        grads_down.reshape(LAYERS, hidden_local, model_width),
        label_logprob,
        token_count,
    )


def solution(mesh):
    batch, model = mesh.devices.shape
    rest = batch // 2
    fine = Mesh(mesh.devices.reshape(rest, 2, 2, model // 2), ("r", "c", "zh", "zl"))
    dp = ("r", "c")
    mp = ("zh", "zl")
    both = dp + mp
    in_specs = (
        P(both, None),
        P(dp),
        P(dp, None),
        P(),
        P(),
        P(None, None, None, mp),
        P(None, mp, None),
        P(None, None, mp),
        P(None, mp, None),
        P(),
        P(both),
        P(both, None),
    )
    out_specs = (
        P(both, None),
        P(both, None),
        P(),
        P(),
        P(None, None, None, mp),
        P(None, mp, None),
        P(None, None, mp),
        P(None, mp, None),
        P(both),
        P(),
    )

    def body(*args):
        return local(*args, rest=rest)

    return jax.shard_map(body, mesh=fine, in_specs=in_specs, out_specs=out_specs, check_vma=False)
```
